32 devices in a mesh: dp: 2 (over x), ctx: 8 (over z, y), tp: 2 (over core).
Axes of the slice: x: 2, y: 2, z: 4, core: 2. Of those that a mesh axis runs over, the one named last changes fastest.
Arguments:
- inputs: bfloat16 [2, 4096, 1024], P('dp', 'tp', 'ctx'), may hold values from -6 to 6
- gate: bfloat16 [2, 4096, 1024], P('dp', 'tp', 'ctx'), may hold values from -6 to 6
- grad_out: bfloat16 [2, 4096, 1024], P('dp', 'tp', 'ctx'), may hold values from -0.125 to 0.125
- filters: float32 [4096, 1024], P('tp', 'ctx'), may hold values from -6 to 6
Outputs:
- grad_inputs: bfloat16 [2, 4096, 1024], P('dp', 'tp', 'ctx')
- grad_gate: bfloat16 [2, 4096, 1024], P('dp', 'tp', 'ctx')
- grad_filters: float32 [4096, 1024], P('tp', 'ctx')
The draws below stay inside these ranges and needn't reach their ends.
All inputs are finite; a program needn't handle non-finite values.
Results may differ from the reference program's by a relative error of at most 0.001.
Values may be sent and summed in bfloat16 or wider, within the bound.
A program may use at most 128 MiB of HBM per device.

```python
import jax
import jax.numpy as jnp
from jax import lax

CHANNELS = 4096
LENGTH = 1024
BATCH = 2


def level_of(own_key, shape, cuts, least, largest):
    factor_of, own = 1.0, jax.random.fold_in(own_key, 6)
    for dim, blocks in cuts:
        draws = jnp.exp(jax.random.uniform(jax.random.fold_in(own, dim), (blocks,), jnp.float32, least / len(cuts), largest / len(cuts)))
        factor_of = factor_of * jnp.repeat(draws, shape[dim] // blocks).reshape([-1 if axis == dim else 1 for axis in range(len(shape))])
    return factor_of


def noise(stream_key, dims, width, bound, cuts=(), kind=jnp.bfloat16):
    factor_of = level_of(stream_key, dims, cuts, -0.22, 0.18) if cuts else 1.0
    values = jax.random.normal(stream_key, dims, jnp.float32) * width * factor_of
    return jnp.minimum(jnp.maximum(values, -bound), bound).astype(kind)


def setup_inputs(seed: int = 0) -> dict:
    seeds = jax.random.split(jax.random.key(seed), 5)
    inputs = noise(seeds[0], (BATCH, CHANNELS, LENGTH), 1.0, 6.0, ((0, 2), (1, 2), (2, 8)))
    gate = noise(seeds[1], (BATCH, CHANNELS, LENGTH), 1.0, 6.0, ((0, 2), (1, 2), (2, 8)))
    grad_out = noise(seeds[2], (BATCH, CHANNELS, LENGTH), (1.0 / (2 * LENGTH) ** 0.5), 0.125, ((0, 2), (1, 2), (2, 8)))
    filters = noise(seeds[3], (CHANNELS, LENGTH), 1.0, 6.0, ((0, 2), (1, 8)), jnp.float32)
    return {"inputs": inputs, "gate": gate, "grad_out": grad_out, "filters": filters}


def reference(inputs, gate, grad_out, filters):
    seq_count, channels, length = inputs.shape
    block_width = min(512, channels)
    blocks = channels // block_width
    padded_len = 2 * length

    def regroup(array):
        return jnp.swapaxes(array.reshape(seq_count, blocks, block_width, length), 0, 1)

    def one_block(pieces):
        signal, gating, upstream, kernel = pieces
        signal = signal.astype(jnp.float32)
        upstream = upstream.astype(jnp.float32)
        product = upstream * gating.astype(jnp.float32)
        kernel_spec = jnp.fft.rfft(kernel.astype(jnp.float32), n=padded_len, axis=-1)
        signal_spec = jnp.fft.rfft(signal, n=padded_len, axis=-1)
        product_spec = jnp.fft.rfft(product, n=padded_len, axis=-1)
        response = jnp.fft.irfft(kernel_spec[None] * signal_spec, n=padded_len, axis=-1)[..., :length]
        back_signal = jnp.fft.irfft(jnp.conj(kernel_spec)[None] * product_spec, n=padded_len, axis=-1)[..., :length]
        lag_terms = jnp.fft.irfft(jnp.conj(signal_spec) * product_spec, n=padded_len, axis=-1)[..., :length]
        filter_grad = jnp.sum(lag_terms, axis=0).astype(jnp.float32)
        gate_grad = (upstream * response).astype(jnp.bfloat16)
        return back_signal.astype(jnp.bfloat16), gate_grad, filter_grad

    results = lax.map(one_block, (regroup(inputs), regroup(gate), regroup(grad_out), filters.reshape(blocks, block_width, length)))
    grad_inputs = jnp.swapaxes(results[0], 0, 1).reshape(seq_count, channels, length)
    grad_gate = jnp.swapaxes(results[1], 0, 1).reshape(seq_count, channels, length)
    grad_filters = results[2].reshape(channels, length)
    return (grad_inputs, grad_gate, grad_filters)
```

```python
import math
from functools import partial
from types import SimpleNamespace

import jax
import jax.numpy as jnp
import numpy as np
from jax import lax
from jax.experimental import pallas as pl
from jax.experimental.pallas import tpu as pltpu
from jax.sharding import PartitionSpec as P

BF16 = jnp.bfloat16
F32 = jnp.float32
PARTS = 4
SPAN = 250.0
TINY = 1e-35
MESH = pl.DeviceIdType.MESH


def tables(groups, width):
    outer = 2 * groups
    total = outer * width
    freqs = groups + 1
    k1 = np.arange(freqs)[:, None, None]
    b = np.arange(width)[None, :, None]
    k2 = np.arange(width)[None, None, :]
    angle = 2.0 * math.pi * ((b * (k1 + outer * k2)) % total) / total
    cosine, sine = np.cos(angle), -np.sin(angle)
    top = np.concatenate([cosine, sine], axis=2)
    bottom = np.concatenate([-sine, cosine], axis=2)
    matrix = np.concatenate([top, bottom], axis=1).astype(np.float32)
    high = matrix.astype(BF16)
    low = (matrix - high.astype(np.float32)).astype(BF16)
    phase = 2.0 * math.pi * ((np.arange(freqs)[:, None] * np.arange(groups)[None, :]) % outer) / outer
    weight = np.full((freqs, 1), 2.0)
    weight[0] = weight[-1] = 1.0
    weight = weight / total
    coef = np.stack([np.cos(phase), -np.sin(phase), weight * np.cos(phase), -weight * np.sin(phase)], axis=1)
    return high, low, coef.reshape(freqs * 4, groups).astype(np.float32)


def split(value):
    high = value.astype(BF16)
    return high, (value - high.astype(F32)).astype(BF16)


def encode(value):
    peak = jnp.maximum(jnp.max(jnp.abs(value), axis=1, keepdims=True), TINY)
    size = jnp.exp2(jnp.abs(value) * (SPAN / peak) - SPAN / 2)
    return jnp.where(value < 0, -size, size).astype(BF16), peak


def decode(sent, peak):
    sent = sent.astype(F32)
    size = (jnp.log2(jnp.abs(sent)) + SPAN / 2) * (peak * (1.0 / SPAN))
    return jnp.where(sent < 0, -size, size)


def diagonal(rows, base):
    lane = lax.broadcasted_iota(jnp.int32, (rows, 128), 1)
    return lane == lax.broadcasted_iota(jnp.int32, (rows, 128), 0) + base


def collect(peak, base):
    return jnp.sum(jnp.where(diagonal(peak.shape[0], base), peak, 0.0), axis=0, keepdims=True)


def spread(line, rows, base):
    return jnp.sum(jnp.where(diagonal(rows, base), line, 0.0), axis=1, keepdims=True)


def buffers(groups, parts, owned, width):
    chunk = owned // parts
    slim = chunk // 2
    block = max(16, slim)
    tall = 2 * chunk + block
    freqs = groups + 1

    def vm(*shape, kind=BF16):
        return pltpu.VMEM(shape, kind)

    def dma(*shape):
        return pltpu.SemaphoreType.DMA(shape)

    lines = (parts, groups, 1, 128)
    return dict(
        mh=vm(freqs, 2 * width, 2 * width),
        ml=vm(freqs, 2 * width, 2 * width),
        dy=vm(groups, owned, width),
        gate=vm(groups, owned, width),
        fin=vm(parts, groups, slim, width, kind=F32),
        stage=vm(parts, groups, tall, width),
        recv=vm(parts, groups, tall, width),
        other=vm(parts, groups, block, width),
        peaks=vm(groups, 8, 128, kind=F32),
        peaks_in=vm(groups, 8, 128, kind=F32),
        peaks_other=vm(groups, 8, 128, kind=F32),
        sig=vm(3, groups, chunk, width, kind=F32),
        acc=vm(3, groups, chunk, width, kind=F32),
        a_hi=vm(3 * chunk, 2 * width),
        a_lo=vm(3 * chunk, 2 * width),
        spec=vm(3 * chunk, 2 * width, kind=F32),
        gi=vm(parts, groups, chunk, width),
        resp=vm(parts, groups, chunk, width),
        resp_in=vm(parts, groups, chunk, width),
        gf=vm(parts, groups, chunk, width, kind=F32),
        inbox=vm(parts, groups, slim, width, kind=F32),
        taps=vm(parts, groups, block, width),
        taps_in=vm(parts, groups, block, width),
        taps_other=vm(parts, groups, block, width),
        lines=vm(*lines, kind=F32),
        lines_in=vm(*lines, kind=F32),
        lines_other=vm(*lines, kind=F32),
        gg_out=vm(groups, owned, width),
        gf_out=vm(groups, owned, width, kind=F32),
        load_sem=dma(4),
        x_sem=dma(parts),
        f_sem=dma(parts),
        stage_send=dma(),
        stage_recv=dma(parts),
        other_send=dma(),
        other_recv=dma(parts),
        peaks_send=dma(),
        peaks_recv=dma(),
        peaks_other_send=dma(),
        peaks_other_recv=dma(),
        gi_send=dma(),
        gi_recv=dma(parts),
        resp_send=dma(),
        resp_recv=dma(parts),
        trade_send=dma(),
        trade_recv=dma(parts),
        taps_send=dma(),
        taps_recv=dma(parts),
        lines_send=dma(),
        lines_recv=dma(parts),
        taps_other_send=dma(),
        taps_other_recv=dma(parts),
        lines_other_send=dma(),
        lines_other_recv=dma(parts),
        gg_sem=dma(parts),
        gf_sem=dma(parts),
    )


def fused_kernel(groups, parts, names, coef, high_ref, low_ref, f_ref, x_ref, dy_ref, gate_ref, ogf_ref, ogi_ref, ogg_ref, *scratch):
    m = SimpleNamespace(**dict(zip(names, scratch)))
    owned, width = f_ref.shape[1:]
    chunk = owned // parts
    slim = chunk // 2
    block = m.other.shape[2]
    rows = min(32, chunk)
    me, dp = lax.axis_index("ctx"), lax.axis_index("dp")
    twin = 1 - dp

    def part(q):
        return pl.ds(q * chunk, chunk)

    def remote(source, target, send, recv, device):
        return pltpu.make_async_remote_copy(
            src_ref=source, dst_ref=target, send_sem=send, recv_sem=recv, device_id=device, device_id_type=MESH
        )

    def local(source, target, sem):
        return pltpu.make_async_copy(source, target, sem)

    def settle(ref, sem):
        pltpu.make_async_copy(ref, ref, sem).wait()

    def peers(body):
        def run(o, _):
            body(lax.rem(me + o, groups))
            return 0

        lax.fori_loop(1, groups, run, 0)

    def spray(source, target, send, recv):
        peers(lambda to: remote(source(to), target, send, recv, {"ctx": to}).start())
        local(source(me), target, recv).start()

    def greet():
        barrier = pltpu.get_barrier_semaphore()
        peers(lambda to: pl.semaphore_signal(barrier, inc=1, device_id={"ctx": to}, device_id_type=MESH))
        pl.semaphore_signal(barrier, inc=1, device_id={"dp": twin}, device_id_type=MESH)
        return lambda: pl.semaphore_wait(barrier, groups)

    def loads():
        return (
            local(dy_ref, m.dy, m.load_sem.at[0]),
            local(gate_ref, m.gate, m.load_sem.at[1]),
            *(
                local(f_ref.at[:, pl.ds(pl.multiple_of(q * chunk + dp * slim, slim), slim)], m.fin.at[q], m.f_sem.at[q])
                for q in range(parts)
            ),
            *(local(x_ref.at[:, part(q)], m.stage.at[q, :, pl.ds(0, chunk)], m.x_sem.at[q]) for q in range(parts)),
        )

    def tables_in():
        return local(high_ref, m.mh, m.load_sem.at[2]), local(low_ref, m.ml, m.load_sem.at[3])

    def prepare(a, _):
        found = []
        for q in range(parts):
            line = jnp.zeros((1, 128), F32)
            for at in range(0, chunk, rows):
                here = pl.ds(q * chunk + at, rows)
                sent, peak = encode(m.dy[a, here, :].astype(F32) * m.gate[a, here, :].astype(F32))
                m.stage[q, a, pl.ds(chunk + at, rows), :] = sent
                line = line + collect(peak, at)
            value = m.fin[q, a]
            if block > slim:
                value = jnp.concatenate([value, jnp.zeros((block - slim, width), F32)], axis=0)
            sent, peak = encode(value)
            m.stage[q, a, pl.ds(2 * chunk, block), :] = sent
            found.append(line + collect(peak, chunk))
        if parts < 8:
            found.append(jnp.zeros((8 - parts, 128), F32))
        m.peaks[a] = jnp.concatenate(found, axis=0)
        return 0

    def pass_filters(q):
        settle(m.recv.at[q], m.stage_recv.at[q])
        remote(
            m.recv.at[q, :, pl.ds(2 * chunk, block)], m.other.at[q], m.other_send, m.other_recv.at[q], {"dp": twin}
        ).start()

    def by_rows(body):
        def run(r, _):
            body(pl.multiple_of(r * rows, rows))
            return 0

        lax.fori_loop(0, chunk // rows, run, 0)

    def fill(q):
        def signals(at):
            here = pl.ds(at, rows)
            for a in range(groups):
                m.sig[0, a, here, :] = m.recv[q, a, here, :].astype(F32)
                peak = spread(m.peaks_in[a, pl.ds(q, 1), :], rows, at)
                m.sig[1, a, here, :] = decode(m.recv[q, a, pl.ds(pl.multiple_of(chunk + at, rows), rows), :], peak)
                for s in range(3):
                    m.acc[s, a, here, :] = jnp.zeros((rows, width), F32)

        def taps(source, lines, which):
            here = pl.ds(pl.multiple_of(which * slim, slim), slim)

            def one(a, _):
                value = decode(source(a), spread(lines[a, pl.ds(q, 1), :], block, chunk))
                m.sig[2, a, here, :] = value[:slim]
                return 0

            lax.fori_loop(0, groups, one, 0)

        by_rows(signals)
        taps(lambda a: m.recv[q, a, pl.ds(2 * chunk, block), :], m.peaks_in, dp)
        if q == 0:
            settle(m.peaks_other, m.peaks_other_recv)
        settle(m.other.at[q], m.other_recv.at[q])
        taps(lambda a: m.other[q, a], m.peaks_other, twin)

    def frequency(k, _):
        base = k * 4

        def put(s, at, real, imag):
            to = pl.ds(pl.multiple_of(at + s * chunk, rows), rows)
            m.a_hi[to, :width], m.a_lo[to, :width] = split(real)
            m.a_hi[to, width:], m.a_lo[to, width:] = split(imag)

        def take(s, at):
            to = pl.ds(pl.multiple_of(at + s * chunk, rows), rows)
            return m.spec[to, :width], m.spec[to, width:]

        def forward(at):
            for s in range(3):
                real = imag = None
                for a in range(groups):
                    value = m.sig[s, a, pl.ds(at, rows), :]
                    re, im = value * coef[base, a], value * coef[base + 1, a]
                    real = re if real is None else real + re
                    imag = im if imag is None else imag + im
                put(s, at, real, imag)

        def multiply(contract):
            dims = (((1,), (contract,)), ((), ()))
            dot = partial(lax.dot_general, dimension_numbers=dims, preferred_element_type=F32)
            high, low = m.a_hi[...], m.a_lo[...]
            m.spec[...] = dot(high, m.mh[k]) + dot(low, m.mh[k]) + dot(high, m.ml[k])

        def pointwise(at):
            (xr, xi), (pr, pi), (fr, fi) = take(0, at), take(1, at), take(2, at)
            put(0, at, fr * xr - fi * xi, fr * xi + fi * xr)
            put(1, at, fr * pr + fi * pi, fr * pi - fi * pr)
            put(2, at, xr * pr + xi * pi, xr * pi - xi * pr)

        def inverse(at):
            for s in range(3):
                real, imag = take(s, at)
                for a in range(groups):
                    m.acc[s, a, pl.ds(at, rows), :] += real * coef[base + 2, a] + imag * coef[base + 3, a]

        by_rows(forward)
        multiply(0)
        by_rows(pointwise)
        multiply(1)
        by_rows(inverse)
        return 0

    def finish(q):
        def one(a, _):
            line = jnp.zeros((1, 128), F32)
            for at in range(0, chunk, rows):
                here = pl.ds(at, rows)
                sent, peak = encode(m.acc[0, a, here, :])
                m.resp[q, a, here, :] = sent
                line = line + collect(peak, at)
                m.gi[q, a, here, :] = m.acc[1, a, here, :].astype(BF16)
                m.gf[q, a, here, :] = m.acc[2, a, here, :]
            m.lines[q, a] = line
            return 0

        lax.fori_loop(0, groups, one, 0)

    def ship(q):
        remote(
            m.gf.at[q, :, pl.ds(pl.multiple_of(twin * slim, slim), slim)],
            m.inbox.at[q],
            m.trade_send,
            m.trade_recv.at[q],
            {"dp": twin},
        ).start()
        spray(lambda to: m.gi.at[q, to], ogi_ref.at[me, part(q)], m.gi_send, m.gi_recv.at[q])
        spray(lambda to: m.resp.at[q, to], m.resp_in.at[q, me], m.resp_send, m.resp_recv.at[q])

    def combine(q):
        settle(m.inbox.at[q], m.trade_recv.at[q])

        def one(a, _):
            value = m.gf[q, a, pl.ds(pl.multiple_of(dp * slim, slim), slim), :] + m.inbox[q, a]
            if block > slim:
                value = jnp.concatenate([value, jnp.zeros((block - slim, width), F32)], axis=0)
            sent, peak = encode(value)
            m.taps[q, a] = sent
            m.lines[q, a] += collect(peak, chunk)
            return 0

        lax.fori_loop(0, groups, one, 0)
        spray(lambda to: m.taps.at[q, to], m.taps_in.at[q, me], m.taps_send, m.taps_recv.at[q])
        spray(lambda to: m.lines.at[q, to], m.lines_in.at[q, me], m.lines_send, m.lines_recv.at[q])

    def pass_taps(q):
        settle(m.taps_in.at[q], m.taps_recv.at[q])
        settle(m.lines_in.at[q], m.lines_recv.at[q])
        remote(m.taps_in.at[q], m.taps_other.at[q], m.taps_other_send, m.taps_other_recv.at[q], {"dp": twin}).start()
        remote(m.lines_in.at[q], m.lines_other.at[q], m.lines_other_send, m.lines_other_recv.at[q], {"dp": twin}).start()

    def gate_grad(q):
        settle(m.resp_in.at[q], m.resp_recv.at[q])

        def one(a, _):
            for at in range(0, chunk, rows):
                value = decode(m.resp_in[q, a, pl.ds(at, rows), :], spread(m.lines_in[q, a], rows, at))
                here = pl.ds(q * chunk + at, rows)
                m.gg_out[a, here, :] = (m.dy[a, here, :].astype(F32) * value).astype(BF16)
            return 0

        lax.fori_loop(0, groups, one, 0)
        local(m.gg_out.at[:, part(q)], ogg_ref.at[:, part(q)], m.gg_sem.at[q]).start()

    def taps_out(q, source, lines, which):
        here = pl.ds(pl.multiple_of(q * chunk + which * slim, slim), slim)

        def one(a, _):
            m.gf_out[a, here, :] = decode(source[q, a], spread(lines[q, a], block, chunk))[:slim]
            return 0

        lax.fori_loop(0, groups, one, 0)

    def close_taps(q):
        settle(m.taps_other.at[q], m.taps_other_recv.at[q])
        settle(m.lines_other.at[q], m.lines_other_recv.at[q])
        taps_out(q, m.taps_other, m.lines_other, twin)
        local(m.gf_out.at[:, part(q)], ogf_ref.at[:, part(q)], m.gf_sem.at[q]).start()

    entered = greet()
    for copy in (*loads(), *tables_in()):
        copy.start()
    for copy in loads():
        copy.wait()
    lax.fori_loop(0, groups, prepare, 0)
    entered()
    spray(lambda to: m.peaks.at[to], m.peaks_in.at[me], m.peaks_send, m.peaks_recv)
    for q in range(parts):
        spray(lambda to, q=q: m.stage.at[q, to], m.recv.at[q, me], m.stage_send, m.stage_recv.at[q])
    for copy in tables_in():
        copy.wait()
    settle(m.peaks_in, m.peaks_recv)
    remote(m.peaks_in, m.peaks_other, m.peaks_other_send, m.peaks_other_recv, {"dp": twin}).start()
    pass_filters(0)

    middle = (groups + 1) // 2 + 1
    for q in range(parts):
        fill(q)
        lax.fori_loop(0, middle, frequency, 0)
        if q:
            combine(q - 1)
        lax.fori_loop(middle, groups + 1, frequency, 0)
        if q + 1 < parts:
            pass_filters(q + 1)
        finish(q)
        ship(q)

    last = parts - 1
    early = max(0, last - 1)
    for q in range(early):
        pass_taps(q)
        gate_grad(q)
        taps_out(q, m.taps_in, m.lines_in, dp)
    combine(last)
    for q in range(early, last):
        pass_taps(q)
        gate_grad(q)
        taps_out(q, m.taps_in, m.lines_in, dp)
    for q in range(last):
        close_taps(q)
    pass_taps(last)
    gate_grad(last)
    taps_out(last, m.taps_in, m.lines_in, dp)
    close_taps(last)

    few = pl.ds(0, groups - 1)
    for q in range(parts):
        settle(ogi_ref.at[:, part(q)], m.gi_recv.at[q])
        local(m.gg_out.at[:, part(q)], ogg_ref.at[:, part(q)], m.gg_sem.at[q]).wait()
        local(m.gf_out.at[:, part(q)], ogf_ref.at[:, part(q)], m.gf_sem.at[q]).wait()
    settle(m.stage.at[:, few], m.stage_send)
    settle(m.peaks.at[few], m.peaks_send)
    settle(m.gi.at[:, few], m.gi_send)
    settle(m.resp.at[:, few], m.resp_send)
    settle(m.taps.at[:, few], m.taps_send)
    settle(m.lines.at[:, few], m.lines_send)
    settle(m.other, m.other_send)
    settle(m.peaks_in, m.peaks_other_send)
    settle(m.inbox, m.trade_send)
    settle(m.taps_in, m.taps_other_send)
    settle(m.lines_in, m.lines_other_send)


def fused(f, x, dy, gate):
    groups, owned, width = f.shape
    parts = PARTS if owned % (32 * PARTS) == 0 else 1
    high, low, coef = tables(groups, width)
    anywhere = pl.BlockSpec(memory_space=pl.ANY)
    shape = (groups, owned, width)
    scratch = buffers(groups, parts, owned, width)
    return pl.pallas_call(
        partial(fused_kernel, groups, parts, tuple(scratch)),
        in_specs=[pl.BlockSpec(memory_space=pltpu.SMEM)] + [anywhere] * 6,
        out_specs=[anywhere] * 3,
        out_shape=[
            jax.ShapeDtypeStruct(shape, F32),
            jax.ShapeDtypeStruct(shape, BF16),
            jax.ShapeDtypeStruct(shape, BF16),
        ],
        scratch_shapes=list(scratch.values()),
        compiler_params=pltpu.CompilerParams(
            collective_id=0, has_side_effects=True, vmem_limit_bytes=60 * 1024 * 1024
        ),
    )(coef, high, low, f, x, dy, gate)


def shards(inputs, gate, grad_out, filters):
    groups = lax.axis_size("ctx")
    channels, width = inputs.shape[1:]
    owned = channels // groups

    def blocks(array):
        return array.reshape(groups, owned, width)

    gf, gi, gg = fused(*(blocks(v) for v in (filters, inputs, grad_out, gate)))
    return (
        gi.reshape(1, channels, width),
        gg.reshape(1, channels, width),
        gf.reshape(channels, width),
    )


def solution(mesh):
    placed = (P("dp", "tp", "ctx"), P("dp", "tp", "ctx"), P("dp", "tp", "ctx"), P("tp", "ctx"))
    return jax.shard_map(
        shards,
        mesh=mesh,
        in_specs=placed,
        out_specs=(P("dp", "tp", "ctx"), P("dp", "tp", "ctx"), P("tp", "ctx")),
        check_vma=False,
    )
```

```python
import math
from functools import partial
from types import SimpleNamespace

import jax
import jax.numpy as jnp
import numpy as np
from jax import lax
from jax.experimental import pallas as pl
from jax.experimental.pallas import tpu as pltpu
from jax.sharding import PartitionSpec as P

BF16 = jnp.bfloat16
F32 = jnp.float32
PARTS = 4
SPAN = 250.0
TINY = 1e-35
MESH = pl.DeviceIdType.MESH


def tables(groups, width):
    outer = 2 * groups
    total = outer * width
    freqs = groups + 1
    k1 = np.arange(freqs)[:, None, None]
    b = np.arange(width)[None, :, None]
    k2 = np.arange(width)[None, None, :]
    angle = 2.0 * math.pi * ((b * (k1 + outer * k2)) % total) / total
    cosine, sine = np.cos(angle), -np.sin(angle)
    top = np.concatenate([cosine, sine], axis=2)
    bottom = np.concatenate([-sine, cosine], axis=2)
    matrix = np.concatenate([top, bottom], axis=1).astype(np.float32)
    high = matrix.astype(BF16)
    low = (matrix - high.astype(np.float32)).astype(BF16)
    return high, low


def rotate(value, turn):
    real, imag = value
    eighth = round(turn * 8) % 8 if abs(turn * 8 - round(turn * 8)) < 1e-9 else None
    if eighth == 0:
        return value
    if eighth == 2:
        return -imag, real
    if eighth == 4:
        return -real, -imag
    if eighth == 6:
        return imag, -real
    cosine, sine = math.cos(2.0 * math.pi * turn), math.sin(2.0 * math.pi * turn)
    return real * cosine - imag * sine, real * sine + imag * cosine


def complex_dft(values, sign):
    count = len(values)
    if count == 1:
        return values
    even, odd = complex_dft(values[0::2], sign), complex_dft(values[1::2], sign)
    turned = [rotate(value, sign * i / count) for i, value in enumerate(odd)]
    upper = [(e[0] + t[0], e[1] + t[1]) for e, t in zip(even, turned)]
    lower = [(e[0] - t[0], e[1] - t[1]) for e, t in zip(even, turned)]
    return upper + lower


def odd_dft(values):
    count = len(values)
    if count == 1:
        return [(values[0], None)]
    half = count // 2
    pairs = [rotate((values[i], -values[i + half]), -i / (2 * count)) for i in range(half)]
    found = complex_dft(pairs, -1)
    out = []
    for k in range(1, count, 2):
        if k % 4 == 1:
            out.append(found[(k - 1) // 4])
        else:
            real, imag = found[(2 * count - k - 1) // 4]
            out.append((real, -imag))
    return out


def weave(even, odd):
    out = []
    for i, value in enumerate(even):
        out.append(value)
        if i < len(odd):
            out.append(odd[i])
    return out


def real_dft(values):
    count = len(values)
    if count == 1:
        return [(values[0], None)]
    half = count // 2
    sums = [values[i] + values[i + half] for i in range(half)]
    gaps = [values[i] - values[i + half] for i in range(half)]
    return weave(real_dft(sums), odd_dft(gaps))


def padded_dft(values):
    return weave(real_dft(values), odd_dft(values))


def odd_dft_back(values, count):
    if count == 1:
        return [values[0][0]]
    half = count // 2
    found = []
    for i in range(half):
        k = 4 * i + 1
        if k < count:
            found.append(values[(k - 1) // 2])
        else:
            real, imag = values[(2 * count - k - 1) // 2]
            found.append((real, -imag))
    turned = [rotate(value, i / (2 * count)) for i, value in enumerate(complex_dft(found, 1))]
    return [value[0] for value in turned] + [-value[1] for value in turned]


def real_dft_back(values, count):
    if count == 1:
        return [values[0][0]]
    sums = real_dft_back(values[0::2], count // 2)
    gaps = odd_dft_back(values[1::2], count // 2)
    return [s + g for s, g in zip(sums, gaps)] + [s - g for s, g in zip(sums, gaps)]


def padded_dft_back(values, count):
    whole = real_dft_back(values[0::2], count)
    return [w + o for w, o in zip(whole, odd_dft_back(values[1::2], count))]


def split(value):
    high = value.astype(BF16)
    return high, (value - high.astype(F32)).astype(BF16)


def encode(value):
    peak = jnp.maximum(jnp.max(jnp.abs(value), axis=1, keepdims=True), TINY)
    size = jnp.exp2(jnp.abs(value) * (SPAN / peak) - SPAN / 2)
    return jnp.where(value < 0, -size, size).astype(BF16), peak


def decode(sent, peak):
    sent = sent.astype(F32)
    size = (jnp.log2(jnp.abs(sent)) + SPAN / 2) * (peak * (1.0 / SPAN))
    return jnp.where(sent < 0, -size, size)


def diagonal(rows, base):
    lane = lax.broadcasted_iota(jnp.int32, (rows, 128), 1)
    return lane == lax.broadcasted_iota(jnp.int32, (rows, 128), 0) + base


def collect(peak, base):
    return jnp.sum(jnp.where(diagonal(peak.shape[0], base), peak, 0.0), axis=0, keepdims=True)


def spread(line, rows, base):
    return jnp.sum(jnp.where(diagonal(rows, base), line, 0.0), axis=1, keepdims=True)


def buffers(groups, parts, owned, width):
    chunk = owned // parts
    slim = chunk // 2
    block = max(16, slim)
    tall = 2 * chunk + block
    freqs = groups + 1

    def vm(*shape, kind=BF16):
        return pltpu.VMEM(shape, kind)

    def dma(*shape):
        return pltpu.SemaphoreType.DMA(shape)

    lines = (parts, groups, 1, 128)
    return dict(
        mh=vm(freqs, 2 * width, 2 * width),
        ml=vm(freqs, 2 * width, 2 * width),
        dy=vm(groups, owned, width),
        gate=vm(groups, owned, width),
        fin=vm(parts, groups, slim, width, kind=F32),
        stage=vm(parts, groups, tall, width),
        recv=vm(parts, groups, tall, width),
        other=vm(parts, groups, block, width),
        peaks=vm(groups, 8, 128, kind=F32),
        peaks_in=vm(groups, 8, 128, kind=F32),
        peaks_other=vm(groups, 8, 128, kind=F32),
        sig=vm(groups, chunk, width, kind=F32),
        a_hi=vm(freqs, 3 * chunk, 2 * width),
        a_lo=vm(freqs, 3 * chunk, 2 * width),
        b_hi=vm(freqs, 3 * chunk, 2 * width),
        b_lo=vm(freqs, 3 * chunk, 2 * width),
        spec=vm(freqs, 3 * chunk, 2 * width, kind=F32),
        gi=vm(parts, groups, chunk, width),
        resp=vm(parts, groups, chunk, width),
        resp_in=vm(parts, groups, chunk, width),
        gf=vm(parts, groups, chunk, width, kind=F32),
        inbox=vm(parts, groups, slim, width, kind=F32),
        taps=vm(parts, groups, block, width),
        taps_in=vm(parts, groups, block, width),
        taps_other=vm(parts, groups, block, width),
        lines=vm(*lines, kind=F32),
        lines_in=vm(*lines, kind=F32),
        lines_other=vm(*lines, kind=F32),
        gg_out=vm(groups, owned, width),
        gf_out=vm(groups, owned, width, kind=F32),
        load_sem=dma(4),
        x_sem=dma(parts),
        f_sem=dma(parts),
        stage_send=dma(),
        stage_recv=dma(parts),
        other_send=dma(),
        other_recv=dma(parts),
        peaks_send=dma(),
        peaks_recv=dma(),
        peaks_other_send=dma(),
        peaks_other_recv=dma(),
        gi_send=dma(),
        gi_recv=dma(parts),
        resp_send=dma(),
        resp_recv=dma(parts),
        trade_send=dma(),
        trade_recv=dma(parts),
        taps_send=dma(),
        taps_recv=dma(parts),
        lines_send=dma(),
        lines_recv=dma(parts),
        taps_other_send=dma(),
        taps_other_recv=dma(parts),
        lines_other_send=dma(),
        lines_other_recv=dma(parts),
        gg_sem=dma(parts),
        gf_sem=dma(parts),
    )


def fused_kernel(groups, parts, names, high_ref, low_ref, f_ref, x_ref, dy_ref, gate_ref, ogf_ref, ogi_ref, ogg_ref, *scratch):
    m = SimpleNamespace(**dict(zip(names, scratch)))
    owned, width = f_ref.shape[1:]
    chunk = owned // parts
    slim = chunk // 2
    block = m.other.shape[2]
    rows = min(32, chunk)
    me, dp = lax.axis_index("ctx"), lax.axis_index("dp")
    twin = 1 - dp
    unit = 1.0 / (groups * width)

    def part(q):
        return pl.ds(q * chunk, chunk)

    def remote(source, target, send, recv, device):
        return pltpu.make_async_remote_copy(
            src_ref=source, dst_ref=target, send_sem=send, recv_sem=recv, device_id=device, device_id_type=MESH
        )

    def local(source, target, sem):
        return pltpu.make_async_copy(source, target, sem)

    def settle(ref, sem):
        pltpu.make_async_copy(ref, ref, sem).wait()

    def peers(body):
        def run(o, _):
            body(lax.rem(me + o, groups))
            return 0

        lax.fori_loop(1, groups, run, 0)

    def spray(source, target, send, recv):
        peers(lambda to: remote(source(to), target, send, recv, {"ctx": to}).start())
        local(source(me), target, recv).start()

    def greet():
        barrier = pltpu.get_barrier_semaphore()
        peers(lambda to: pl.semaphore_signal(barrier, inc=1, device_id={"ctx": to}, device_id_type=MESH))
        pl.semaphore_signal(barrier, inc=1, device_id={"dp": twin}, device_id_type=MESH)
        return lambda: pl.semaphore_wait(barrier, groups)

    def loads():
        return (
            local(dy_ref, m.dy, m.load_sem.at[0]),
            local(gate_ref, m.gate, m.load_sem.at[1]),
            *(
                local(f_ref.at[:, pl.ds(pl.multiple_of(q * chunk + dp * slim, slim), slim)], m.fin.at[q], m.f_sem.at[q])
                for q in range(parts)
            ),
            *(local(x_ref.at[:, part(q)], m.stage.at[q, :, pl.ds(0, chunk)], m.x_sem.at[q]) for q in range(parts)),
        )

    def tables_in():
        return local(high_ref, m.mh, m.load_sem.at[2]), local(low_ref, m.ml, m.load_sem.at[3])

    def prepare(a, _):
        found = []
        for q in range(parts):
            line = jnp.zeros((1, 128), F32)
            for at in range(0, chunk, rows):
                here = pl.ds(q * chunk + at, rows)
                sent, peak = encode(m.dy[a, here, :].astype(F32) * m.gate[a, here, :].astype(F32))
                m.stage[q, a, pl.ds(chunk + at, rows), :] = sent
                line = line + collect(peak, at)
            value = m.fin[q, a]
            if block > slim:
                value = jnp.concatenate([value, jnp.zeros((block - slim, width), F32)], axis=0)
            sent, peak = encode(value)
            m.stage[q, a, pl.ds(2 * chunk, block), :] = sent
            found.append(line + collect(peak, chunk))
        if parts < 8:
            found.append(jnp.zeros((8 - parts, 128), F32))
        m.peaks[a] = jnp.concatenate(found, axis=0)
        return 0

    def pass_filters(q):
        settle(m.recv.at[q], m.stage_recv.at[q])
        remote(
            m.recv.at[q, :, pl.ds(2 * chunk, block)], m.other.at[q], m.other_send, m.other_recv.at[q], {"dp": twin}
        ).start()

    def by_rows(body):
        def run(r, _):
            body(pl.multiple_of(r * 16, 16))
            return 0

        lax.fori_loop(0, chunk // 16, run, 0)

    def put(high, low, k, s, at, real, imag):
        to = pl.ds(pl.multiple_of(at + s * chunk, 16), 16)
        if imag is None:
            imag = jnp.zeros_like(real)
        high[k, to, :width], low[k, to, :width] = split(real)
        high[k, to, width:], low[k, to, width:] = split(imag)

    def analyse(s, at, values):
        for k, (real, imag) in enumerate(padded_dft(values)):
            put(m.a_hi, m.a_lo, k, s, at, real, imag)

    def fill(q):
        def signals(at):
            here = pl.ds(at, 16)
            analyse(0, at, [m.recv[q, a, here, :].astype(F32) for a in range(groups)])
            there = pl.ds(pl.multiple_of(chunk + at, 16), 16)
            analyse(
                1,
                at,
                [
                    decode(m.recv[q, a, there, :], spread(m.peaks_in[a, pl.ds(q, 1), :], 16, at) )
                    for a in range(groups)
                ],
            )

        def taps(source, lines, which):
            here = pl.ds(pl.multiple_of(which * slim, slim), slim)
            for a in range(groups):
                peak = spread(lines[a, pl.ds(q, 1), :], block, chunk)
                m.sig[a, here, :] = decode(source(a), peak)[:slim]

        by_rows(signals)
        taps(lambda a: m.recv[q, a, pl.ds(2 * chunk, block), :], m.peaks_in, dp)
        if q == 0:
            settle(m.peaks_other, m.peaks_other_recv)
        settle(m.other.at[q], m.other_recv.at[q])
        taps(lambda a: m.other[q, a], m.peaks_other, twin)
        by_rows(lambda at: analyse(2, at, [m.sig[a, pl.ds(at, 16), :] for a in range(groups)]))

    def frequency(k):
        def multiply(high, low, contract):
            dims = (((1,), (contract,)), ((), ()))
            dot = partial(lax.dot_general, dimension_numbers=dims, preferred_element_type=F32)
            high, low = high[k], low[k]
            return dot(high, m.mh[k]) + dot(low, m.mh[k]) + dot(high, m.ml[k])

        found = multiply(m.a_hi, m.a_lo, 0)
        (xr, xi), (pr, pi), (fr, fi) = (
            (found[s * chunk : (s + 1) * chunk, :width], found[s * chunk : (s + 1) * chunk, width:]) for s in range(3)
        )
        for s, (real, imag) in enumerate(
            (
                (fr * xr - fi * xi, fr * xi + fi * xr),
                (fr * pr + fi * pi, fr * pi - fi * pr),
                (xr * pr + xi * pi, xr * pi - xi * pr),
            )
        ):
            to = pl.ds(s * chunk, chunk)
            m.b_hi[k, to, :width], m.b_lo[k, to, :width] = split(real)
            m.b_hi[k, to, width:], m.b_lo[k, to, width:] = split(imag)
        m.spec[k] = multiply(m.b_hi, m.b_lo, 1)

    def synthesise(s, at):
        to = pl.ds(pl.multiple_of(at + s * chunk, 16), 16)
        values = [(m.spec[k, to, :width], m.spec[k, to, width:]) for k in range(groups + 1)]
        values[0], values[-1] = ((value[0] * 0.5, None) for value in (values[0], values[-1]))
        return padded_dft_back(values, groups)

    def finish(q):
        m.lines[q] = jnp.zeros((groups, 1, 128), F32)

        def one(at):
            here = pl.ds(at, 16)
            for a, value in enumerate(synthesise(0, at)):
                sent, peak = encode(value * unit)
                m.resp[q, a, here, :] = sent
                m.lines[q, a] += collect(peak, at)
            for a, value in enumerate(synthesise(1, at)):
                m.gi[q, a, here, :] = (value * unit).astype(BF16)
            for a, value in enumerate(synthesise(2, at)):
                m.gf[q, a, here, :] = value * unit

        by_rows(one)

    def ship(q):
        remote(
            m.gf.at[q, :, pl.ds(pl.multiple_of(twin * slim, slim), slim)],
            m.inbox.at[q],
            m.trade_send,
            m.trade_recv.at[q],
            {"dp": twin},
        ).start()
        spray(lambda to: m.gi.at[q, to], ogi_ref.at[me, part(q)], m.gi_send, m.gi_recv.at[q])
        spray(lambda to: m.resp.at[q, to], m.resp_in.at[q, me], m.resp_send, m.resp_recv.at[q])

    def combine(q):
        settle(m.inbox.at[q], m.trade_recv.at[q])

        def one(a, _):
            value = m.gf[q, a, pl.ds(pl.multiple_of(dp * slim, slim), slim), :] + m.inbox[q, a]
            if block > slim:
                value = jnp.concatenate([value, jnp.zeros((block - slim, width), F32)], axis=0)
            sent, peak = encode(value)
            m.taps[q, a] = sent
            m.lines[q, a] += collect(peak, chunk)
            return 0

        lax.fori_loop(0, groups, one, 0)
        spray(lambda to: m.taps.at[q, to], m.taps_in.at[q, me], m.taps_send, m.taps_recv.at[q])
        spray(lambda to: m.lines.at[q, to], m.lines_in.at[q, me], m.lines_send, m.lines_recv.at[q])

    def pass_taps(q):
        settle(m.taps_in.at[q], m.taps_recv.at[q])
        settle(m.lines_in.at[q], m.lines_recv.at[q])
        remote(m.taps_in.at[q], m.taps_other.at[q], m.taps_other_send, m.taps_other_recv.at[q], {"dp": twin}).start()
        remote(m.lines_in.at[q], m.lines_other.at[q], m.lines_other_send, m.lines_other_recv.at[q], {"dp": twin}).start()

    def gate_grad(q):
        settle(m.resp_in.at[q], m.resp_recv.at[q])

        def one(a, _):
            for at in range(0, chunk, rows):
                value = decode(m.resp_in[q, a, pl.ds(at, rows), :], spread(m.lines_in[q, a], rows, at))
                here = pl.ds(q * chunk + at, rows)
                m.gg_out[a, here, :] = (m.dy[a, here, :].astype(F32) * value).astype(BF16)
            return 0

        lax.fori_loop(0, groups, one, 0)
        local(m.gg_out.at[:, part(q)], ogg_ref.at[:, part(q)], m.gg_sem.at[q]).start()

    def taps_out(q, source, lines, which):
        here = pl.ds(pl.multiple_of(q * chunk + which * slim, slim), slim)

        def one(a, _):
            m.gf_out[a, here, :] = decode(source[q, a], spread(lines[q, a], block, chunk))[:slim]
            return 0

        lax.fori_loop(0, groups, one, 0)

    def close_taps(q):
        settle(m.taps_other.at[q], m.taps_other_recv.at[q])
        settle(m.lines_other.at[q], m.lines_other_recv.at[q])
        taps_out(q, m.taps_other, m.lines_other, twin)
        local(m.gf_out.at[:, part(q)], ogf_ref.at[:, part(q)], m.gf_sem.at[q]).start()

    entered = greet()
    for copy in (*loads(), *tables_in()):
        copy.start()
    for copy in loads():
        copy.wait()
    lax.fori_loop(0, groups, prepare, 0)
    entered()
    spray(lambda to: m.peaks.at[to], m.peaks_in.at[me], m.peaks_send, m.peaks_recv)
    for q in range(parts):
        spray(lambda to, q=q: m.stage.at[q, to], m.recv.at[q, me], m.stage_send, m.stage_recv.at[q])
    for copy in tables_in():
        copy.wait()
    settle(m.peaks_in, m.peaks_recv)
    remote(m.peaks_in, m.peaks_other, m.peaks_other_send, m.peaks_other_recv, {"dp": twin}).start()
    pass_filters(0)

    middle = groups // 2
    for q in range(parts):
        fill(q)
        for k in range(groups + 1):
            frequency(k)
            if q and k == middle:
                combine(q - 1)
        if q + 1 < parts:
            pass_filters(q + 1)
        finish(q)
        ship(q)

    last = parts - 1
    early = max(0, last - 1)
    for q in range(early):
        pass_taps(q)
        gate_grad(q)
        taps_out(q, m.taps_in, m.lines_in, dp)
    combine(last)
    for q in range(early, last):
        pass_taps(q)
        gate_grad(q)
        taps_out(q, m.taps_in, m.lines_in, dp)
    for q in range(last):
        close_taps(q)
    pass_taps(last)
    gate_grad(last)
    taps_out(last, m.taps_in, m.lines_in, dp)
    close_taps(last)

    few = pl.ds(0, groups - 1)
    for q in range(parts):
        settle(ogi_ref.at[:, part(q)], m.gi_recv.at[q])
        local(m.gg_out.at[:, part(q)], ogg_ref.at[:, part(q)], m.gg_sem.at[q]).wait()
        local(m.gf_out.at[:, part(q)], ogf_ref.at[:, part(q)], m.gf_sem.at[q]).wait()
    settle(m.stage.at[:, few], m.stage_send)
    settle(m.peaks.at[few], m.peaks_send)
    settle(m.gi.at[:, few], m.gi_send)
    settle(m.resp.at[:, few], m.resp_send)
    settle(m.taps.at[:, few], m.taps_send)
    settle(m.lines.at[:, few], m.lines_send)
    settle(m.other, m.other_send)
    settle(m.peaks_in, m.peaks_other_send)
    settle(m.inbox, m.trade_send)
    settle(m.taps_in, m.taps_other_send)
    settle(m.lines_in, m.lines_other_send)


def fused(f, x, dy, gate):
    groups, owned, width = f.shape
    parts = PARTS if owned % (32 * PARTS) == 0 else 1
    high, low = tables(groups, width)
    anywhere = pl.BlockSpec(memory_space=pl.ANY)
    shape = (groups, owned, width)
    scratch = buffers(groups, parts, owned, width)
    return pl.pallas_call(
        partial(fused_kernel, groups, parts, tuple(scratch)),
        in_specs=[anywhere] * 6,
        out_specs=[anywhere] * 3,
        out_shape=[
            jax.ShapeDtypeStruct(shape, F32),
            jax.ShapeDtypeStruct(shape, BF16),
            jax.ShapeDtypeStruct(shape, BF16),
        ],
        scratch_shapes=list(scratch.values()),
        compiler_params=pltpu.CompilerParams(
            collective_id=0, has_side_effects=True, vmem_limit_bytes=52 * 1024 * 1024
        ),
    )(high, low, f, x, dy, gate)


def shards(inputs, gate, grad_out, filters):
    groups = lax.axis_size("ctx")
    channels, width = inputs.shape[1:]
    owned = channels // groups

    def blocks(array):
        return array.reshape(groups, owned, width)

    gf, gi, gg = fused(*(blocks(v) for v in (filters, inputs, grad_out, gate)))
    return (
        gi.reshape(1, channels, width),
        gg.reshape(1, channels, width),
        gf.reshape(channels, width),
    )


def solution(mesh):
    placed = (P("dp", "tp", "ctx"), P("dp", "tp", "ctx"), P("dp", "tp", "ctx"), P("tp", "ctx"))
    return jax.shard_map(
        shards,
        mesh=mesh,
        in_specs=placed,
        out_specs=(P("dp", "tp", "ctx"), P("dp", "tp", "ctx"), P("tp", "ctx")),
        check_vma=False,
    )
```

```python
import math
from functools import partial
from types import SimpleNamespace

import jax
import jax.numpy as jnp
import numpy as np
from jax import lax
from jax.experimental import pallas as pl
from jax.experimental.pallas import tpu as pltpu
from jax.sharding import PartitionSpec as P

BF16 = jnp.bfloat16
F32 = jnp.float32
PARTS = 4
SPAN = 250.0
TINY = 1e-35
MESH = pl.DeviceIdType.MESH


def tables(groups, width):
    outer = 2 * groups
    total = outer * width
    freqs = groups + 1
    k1 = np.arange(freqs)[:, None, None]
    b = np.arange(width)[None, :, None]
    k2 = np.arange(width)[None, None, :]
    angle = 2.0 * math.pi * ((b * (k1 + outer * k2)) % total) / total
    cosine, sine = np.cos(angle), -np.sin(angle)
    top = np.concatenate([cosine, sine], axis=2)
    bottom = np.concatenate([-sine, cosine], axis=2)
    matrix = np.concatenate([top, bottom], axis=1).astype(np.float32)
    high = matrix.astype(BF16)
    low = (matrix - high.astype(np.float32)).astype(BF16)
    return high, low


def rotate(value, turn):
    real, imag = value
    eighth = round(turn * 8) % 8 if abs(turn * 8 - round(turn * 8)) < 1e-9 else None
    if eighth == 0:
        return value
    if eighth == 2:
        return -imag, real
    if eighth == 4:
        return -real, -imag
    if eighth == 6:
        return imag, -real
    cosine, sine = math.cos(2.0 * math.pi * turn), math.sin(2.0 * math.pi * turn)
    return real * cosine - imag * sine, real * sine + imag * cosine


def complex_dft(values, sign):
    count = len(values)
    if count == 1:
        return values
    even, odd = complex_dft(values[0::2], sign), complex_dft(values[1::2], sign)
    turned = [rotate(value, sign * i / count) for i, value in enumerate(odd)]
    upper = [(e[0] + t[0], e[1] + t[1]) for e, t in zip(even, turned)]
    lower = [(e[0] - t[0], e[1] - t[1]) for e, t in zip(even, turned)]
    return upper + lower


def odd_dft(values):
    count = len(values)
    if count == 1:
        return [(values[0], None)]
    half = count // 2
    pairs = [rotate((values[i], -values[i + half]), -i / (2 * count)) for i in range(half)]
    found = complex_dft(pairs, -1)
    out = []
    for k in range(1, count, 2):
        if k % 4 == 1:
            out.append(found[(k - 1) // 4])
        else:
            real, imag = found[(2 * count - k - 1) // 4]
            out.append((real, -imag))
    return out


def weave(even, odd):
    out = []
    for i, value in enumerate(even):
        out.append(value)
        if i < len(odd):
            out.append(odd[i])
    return out


def real_dft(values):
    count = len(values)
    if count == 1:
        return [(values[0], None)]
    half = count // 2
    sums = [values[i] + values[i + half] for i in range(half)]
    gaps = [values[i] - values[i + half] for i in range(half)]
    return weave(real_dft(sums), odd_dft(gaps))


def padded_dft(values):
    return weave(real_dft(values), odd_dft(values))


def odd_dft_back(values, count):
    if count == 1:
        return [values[0][0]]
    half = count // 2
    found = []
    for i in range(half):
        k = 4 * i + 1
        if k < count:
            found.append(values[(k - 1) // 2])
        else:
            real, imag = values[(2 * count - k - 1) // 2]
            found.append((real, -imag))
    turned = [rotate(value, i / (2 * count)) for i, value in enumerate(complex_dft(found, 1))]
    return [value[0] for value in turned] + [-value[1] for value in turned]


def real_dft_back(values, count):
    if count == 1:
        return [values[0][0]]
    sums = real_dft_back(values[0::2], count // 2)
    gaps = odd_dft_back(values[1::2], count // 2)
    return [s + g for s, g in zip(sums, gaps)] + [s - g for s, g in zip(sums, gaps)]


def padded_dft_back(values, count):
    whole = real_dft_back(values[0::2], count)
    return [w + o for w, o in zip(whole, odd_dft_back(values[1::2], count))]


def split(value):
    high = value.astype(BF16)
    return high, (value - high.astype(F32)).astype(BF16)


def encode(value):
    peak = jnp.maximum(jnp.max(jnp.abs(value), axis=1, keepdims=True), TINY)
    size = jnp.exp2(jnp.abs(value) * (SPAN / peak) - SPAN / 2)
    return jnp.where(value < 0, -size, size).astype(BF16), peak


def decode(sent, peak):
    sent = sent.astype(F32)
    size = (jnp.log2(jnp.abs(sent)) + SPAN / 2) * (peak * (1.0 / SPAN))
    return jnp.where(sent < 0, -size, size)


def diagonal(rows, base):
    lane = lax.broadcasted_iota(jnp.int32, (rows, 128), 1)
    return lane == lax.broadcasted_iota(jnp.int32, (rows, 128), 0) + base


def collect(peak, base):
    return jnp.sum(jnp.where(diagonal(peak.shape[0], base), peak, 0.0), axis=0, keepdims=True)


def spread(line, rows, base):
    return jnp.sum(jnp.where(diagonal(rows, base), line, 0.0), axis=1, keepdims=True)


def buffers(groups, parts, owned, width):
    chunk = owned // parts
    slim = chunk // 2
    block = max(16, slim)
    tall = 2 * chunk + block
    freqs = groups + 1

    def vm(*shape, kind=BF16):
        return pltpu.VMEM(shape, kind)

    def dma(*shape):
        return pltpu.SemaphoreType.DMA(shape)

    lines = (groups, parts, 1, 128)
    taps = (groups, parts * block, width)
    sets = min(parts, 2)
    return dict(
        mh=vm(freqs, 2 * width, 2 * width),
        ml=vm(freqs, 2 * width, 2 * width),
        dy=vm(groups, owned, width),
        gate=vm(groups, owned, width),
        fin=vm(parts, groups, slim, width, kind=F32),
        stage=vm(parts, groups, tall, width),
        recv=vm(parts, groups, tall, width),
        other=vm(parts, groups, block, width),
        peaks=vm(groups, parts, 128, kind=F32),
        peaks_in=vm(groups, parts, 128, kind=F32),
        peaks_other=vm(groups, parts, 128, kind=F32),
        sig=vm(groups, chunk, width, kind=F32),
        a_hi=vm(freqs, 3 * chunk, 2 * width),
        a_lo=vm(freqs, 3 * chunk, 2 * width),
        b_hi=vm(freqs, 3 * chunk, 2 * width),
        b_lo=vm(freqs, 3 * chunk, 2 * width),
        spec=vm(freqs, 3 * chunk, 2 * width, kind=F32),
        gi=vm(groups, owned, width),
        resp=vm(groups, owned, width),
        resp_in=vm(groups, owned, width),
        gf=vm(parts, groups, chunk, width, kind=F32),
        inbox=vm(parts, groups, slim, width, kind=F32),
        taps=vm(*taps),
        taps_in=vm(*taps),
        taps_other=vm(*taps),
        lines=vm(*lines, kind=F32),
        lines_in=vm(*lines, kind=F32),
        lines_other=vm(*lines, kind=F32),
        gg_out=vm(groups, owned, width),
        gf_out=vm(groups, owned, width, kind=F32),
        load_sem=dma(4),
        x_sem=dma(parts),
        f_sem=dma(parts),
        stage_send=dma(),
        stage_recv=dma(parts),
        other_send=dma(),
        other_recv=dma(parts),
        peaks_send=dma(),
        peaks_recv=dma(),
        peaks_other_send=dma(),
        peaks_other_recv=dma(),
        gi_send=dma(),
        gi_recv=dma(),
        resp_send=dma(),
        resp_recv=dma(sets),
        trade_send=dma(),
        trade_recv=dma(parts),
        taps_send=dma(),
        taps_recv=dma(sets),
        lines_send=dma(),
        lines_recv=dma(sets),
        taps_other_send=dma(),
        taps_other_recv=dma(sets),
        lines_other_send=dma(),
        lines_other_recv=dma(sets),
        gg_sem=dma(sets),
        gf_sem=dma(sets),
    )


def fused_kernel(groups, parts, names, high_ref, low_ref, f_ref, x_ref, dy_ref, gate_ref, ogf_ref, ogi_ref, ogg_ref, *scratch):
    m = SimpleNamespace(**dict(zip(names, scratch)))
    owned, width = f_ref.shape[1:]
    chunk = owned // parts
    slim = chunk // 2
    block = m.other.shape[2]
    rows = min(32, chunk)
    me, dp = lax.axis_index("ctx"), lax.axis_index("dp")
    twin = 1 - dp
    sets = ((0, parts - 1), (parts - 1, 1)) if parts > 1 else ((0, 1),)
    unit = 1.0 / (groups * width)

    def part(q):
        return pl.ds(q * chunk, chunk)

    def remote(source, target, send, recv, device):
        return pltpu.make_async_remote_copy(
            src_ref=source, dst_ref=target, send_sem=send, recv_sem=recv, device_id=device, device_id_type=MESH
        )

    def local(source, target, sem):
        return pltpu.make_async_copy(source, target, sem)

    def settle(ref, sem):
        pltpu.make_async_copy(ref, ref, sem).wait()

    def peers(body):
        def run(o, _):
            body(lax.rem(me + o, groups))
            return 0

        lax.fori_loop(1, groups, run, 0)

    def spray(source, target, send, recv):
        peers(lambda to: remote(source(to), target, send, recv, {"ctx": to}).start())
        local(source(me), target, recv).start()

    def greet():
        barrier = pltpu.get_barrier_semaphore()
        peers(lambda to: pl.semaphore_signal(barrier, inc=1, device_id={"ctx": to}, device_id_type=MESH))
        pl.semaphore_signal(barrier, inc=1, device_id={"dp": twin}, device_id_type=MESH)
        return lambda: pl.semaphore_wait(barrier, groups)

    def loads():
        return (
            local(dy_ref, m.dy, m.load_sem.at[0]),
            local(gate_ref, m.gate, m.load_sem.at[1]),
            *(
                local(f_ref.at[:, pl.ds(pl.multiple_of(q * chunk + dp * slim, slim), slim)], m.fin.at[q], m.f_sem.at[q])
                for q in range(parts)
            ),
            *(local(x_ref.at[:, part(q)], m.stage.at[q, :, pl.ds(0, chunk)], m.x_sem.at[q]) for q in range(parts)),
        )

    def tables_in():
        return local(high_ref, m.mh, m.load_sem.at[2]), local(low_ref, m.ml, m.load_sem.at[3])

    def prepare(a, _):
        found = []
        for q in range(parts):
            line = jnp.zeros((1, 128), F32)
            for at in range(0, chunk, rows):
                here = pl.ds(q * chunk + at, rows)
                sent, peak = encode(m.dy[a, here, :].astype(F32) * m.gate[a, here, :].astype(F32))
                m.stage[q, a, pl.ds(chunk + at, rows), :] = sent
                line = line + collect(peak, at)
            value = m.fin[q, a]
            if block > slim:
                value = jnp.concatenate([value, jnp.zeros((block - slim, width), F32)], axis=0)
            sent, peak = encode(value)
            m.stage[q, a, pl.ds(2 * chunk, block), :] = sent
            found.append(line + collect(peak, chunk))
        m.peaks[a] = jnp.concatenate(found, axis=0)
        return 0

    def inward(q):
        spray(lambda to: m.stage.at[q, to], m.recv.at[q, me], m.stage_send, m.stage_recv.at[q])

    def pass_filters(q):
        settle(m.recv.at[q], m.stage_recv.at[q])
        if 1 <= q + 1 < parts:
            inward(q + 1)
        remote(
            m.recv.at[q, :, pl.ds(2 * chunk, block)], m.other.at[q], m.other_send, m.other_recv.at[q], {"dp": twin}
        ).start()

    def by_rows(body):
        def run(r, _):
            body(pl.multiple_of(r * 16, 16))
            return 0

        lax.fori_loop(0, chunk // 16, run, 0)

    def put(high, low, k, s, at, real, imag):
        to = pl.ds(pl.multiple_of(at + s * chunk, 16), 16)
        if imag is None:
            imag = jnp.zeros_like(real)
        high[k, to, :width], low[k, to, :width] = split(real)
        high[k, to, width:], low[k, to, width:] = split(imag)

    def analyse(s, at, values):
        for k, (real, imag) in enumerate(padded_dft(values)):
            put(m.a_hi, m.a_lo, k, s, at, real, imag)

    def fill(q):
        def signals(at):
            here = pl.ds(at, 16)
            analyse(0, at, [m.recv[q, a, here, :].astype(F32) for a in range(groups)])
            there = pl.ds(pl.multiple_of(chunk + at, 16), 16)
            analyse(
                1,
                at,
                [
                    decode(m.recv[q, a, there, :], spread(m.peaks_in[a, pl.ds(q, 1), :], 16, at) )
                    for a in range(groups)
                ],
            )

        def taps(source, lines, which):
            here = pl.ds(pl.multiple_of(which * slim, slim), slim)
            for a in range(groups):
                peak = spread(lines[a, pl.ds(q, 1), :], block, chunk)
                m.sig[a, here, :] = decode(source(a), peak)[:slim]

        by_rows(signals)
        taps(lambda a: m.recv[q, a, pl.ds(2 * chunk, block), :], m.peaks_in, dp)
        if q == 0:
            settle(m.peaks_other, m.peaks_other_recv)
        settle(m.other.at[q], m.other_recv.at[q])
        taps(lambda a: m.other[q, a], m.peaks_other, twin)
        by_rows(lambda at: analyse(2, at, [m.sig[a, pl.ds(at, 16), :] for a in range(groups)]))

    def frequency(k):
        def multiply(high, low, contract):
            dims = (((1,), (contract,)), ((), ()))
            dot = partial(lax.dot_general, dimension_numbers=dims, preferred_element_type=F32)
            high, low = high[k], low[k]
            both = dot(jnp.concatenate([high, low], axis=0), m.mh[k])
            return both[: 3 * chunk] + both[3 * chunk :] + dot(high, m.ml[k])

        found = multiply(m.a_hi, m.a_lo, 0)
        (xr, xi), (pr, pi), (fr, fi) = (
            (found[s * chunk : (s + 1) * chunk, :width], found[s * chunk : (s + 1) * chunk, width:]) for s in range(3)
        )
        for s, (real, imag) in enumerate(
            (
                (fr * xr - fi * xi, fr * xi + fi * xr),
                (fr * pr + fi * pi, fr * pi - fi * pr),
                (xr * pr + xi * pi, xr * pi - xi * pr),
            )
        ):
            to = pl.ds(s * chunk, chunk)
            m.b_hi[k, to, :width], m.b_lo[k, to, :width] = split(real)
            m.b_hi[k, to, width:], m.b_lo[k, to, width:] = split(imag)
        m.spec[k] = multiply(m.b_hi, m.b_lo, 1)

    def synthesise(s, at):
        to = pl.ds(pl.multiple_of(at + s * chunk, 16), 16)
        values = [(m.spec[k, to, :width], m.spec[k, to, width:]) for k in range(groups + 1)]
        values[0], values[-1] = ((value[0] * 0.5, None) for value in (values[0], values[-1]))
        return padded_dft_back(values, groups)

    def finish(q):
        m.lines[:, q] = jnp.zeros((groups, 1, 128), F32)

        def one(at):
            here = pl.ds(pl.multiple_of(q * chunk + at, 16), 16)
            for a, value in enumerate(synthesise(2, at)):
                m.gf[q, a, pl.ds(at, 16), :] = value * unit
            for a, value in enumerate(synthesise(0, at)):
                sent, peak = encode(value * unit)
                m.resp[a, here, :] = sent
                m.lines[a, q] += collect(peak, at)
            for a, value in enumerate(synthesise(1, at)):
                m.gi[a, here, :] = (value * unit).astype(BF16)

        by_rows(one)

    def trade(q):
        remote(
            m.gf.at[q, :, pl.ds(pl.multiple_of(twin * slim, slim), slim)],
            m.inbox.at[q],
            m.trade_send,
            m.trade_recv.at[q],
            {"dp": twin},
        ).start()

    def send_response(g):
        here = span(g)
        spray(lambda to: m.resp.at[to, here], m.resp_in.at[me, here], m.resp_send, m.resp_recv.at[g])

    def send_inputs():
        spray(lambda to: m.gi.at[to], ogi_ref.at[me], m.gi_send, m.gi_recv)

    def combine(q):
        settle(m.inbox.at[q], m.trade_recv.at[q])

        def one(a, _):
            value = m.gf[q, a, pl.ds(pl.multiple_of(dp * slim, slim), slim), :] + m.inbox[q, a]
            if block > slim:
                value = jnp.concatenate([value, jnp.zeros((block - slim, width), F32)], axis=0)
            sent, peak = encode(value)
            m.taps[a, pl.ds(q * block, block), :] = sent
            m.lines[a, q] += collect(peak, chunk)
            return 0

        lax.fori_loop(0, groups, one, 0)

    def some(g):
        first, count = sets[g]
        return pl.ds(first, count)

    def span(g):
        first, count = sets[g]
        return pl.ds(first * chunk, count * chunk)

    def span_taps(g):
        first, count = sets[g]
        return pl.ds(first * block, count * block)

    def send_taps(g):
        here, there = some(g), span_taps(g)
        spray(lambda to: m.lines.at[to, here], m.lines_in.at[me, here], m.lines_send, m.lines_recv.at[g])
        spray(lambda to: m.taps.at[to, there], m.taps_in.at[me, there], m.taps_send, m.taps_recv.at[g])

    def pass_taps(g):
        lines, taps = m.lines_in.at[:, some(g)], m.taps_in.at[:, span_taps(g)]
        settle(lines, m.lines_recv.at[g])
        settle(taps, m.taps_recv.at[g])
        other_lines, other_taps = m.lines_other.at[:, some(g)], m.taps_other.at[:, span_taps(g)]
        remote(lines, other_lines, m.lines_other_send, m.lines_other_recv.at[g], {"dp": twin}).start()
        remote(taps, other_taps, m.taps_other_send, m.taps_other_recv.at[g], {"dp": twin}).start()

    def gg_out(g):
        return local(m.gg_out.at[:, span(g)], ogg_ref.at[:, span(g)], m.gg_sem.at[g])

    def gf_out(g):
        return local(m.gf_out.at[:, span(g)], ogf_ref.at[:, span(g)], m.gf_sem.at[g])

    def gate_grad(g):
        settle(m.resp_in.at[:, span(g)], m.resp_recv.at[g])
        first, count = sets[g]

        def one(a, _):
            for q in range(first, first + count):
                for at in range(0, chunk, rows):
                    here = pl.ds(q * chunk + at, rows)
                    value = decode(m.resp_in[a, here, :], spread(m.lines_in[a, q], rows, at))
                    m.gg_out[a, here, :] = (m.dy[a, here, :].astype(F32) * value).astype(BF16)
            return 0

        lax.fori_loop(0, groups, one, 0)
        gg_out(g).start()

    def taps_out(g, source, lines, which):
        first, count = sets[g]

        def one(a, _):
            for q in range(first, first + count):
                value = decode(source[a, pl.ds(q * block, block), :], spread(lines[a, q], block, chunk))
                here = pl.ds(pl.multiple_of(q * chunk + which * slim, slim), slim)
                m.gf_out[a, here, :] = value[:slim]
            return 0

        lax.fori_loop(0, groups, one, 0)

    def close_taps(g):
        settle(m.taps_other.at[:, span_taps(g)], m.taps_other_recv.at[g])
        settle(m.lines_other.at[:, some(g)], m.lines_other_recv.at[g])
        taps_out(g, m.taps_other, m.lines_other, twin)
        gf_out(g).start()

    entered = greet()
    for copy in (*loads(), *tables_in()):
        copy.start()
    for copy in loads():
        copy.wait()
    lax.fori_loop(0, groups, prepare, 0)
    entered()
    spray(lambda to: m.peaks.at[to], m.peaks_in.at[me], m.peaks_send, m.peaks_recv)
    for q in range(min(1, parts)):
        inward(q)
    for copy in tables_in():
        copy.wait()
    settle(m.peaks_in, m.peaks_recv)
    remote(m.peaks_in, m.peaks_other, m.peaks_other_send, m.peaks_other_recv, {"dp": twin}).start()

    last = parts - 1
    for q in range(parts):
        pass_filters(q)
        if q and q == last:
            send_response(0)
        fill(q)
        for k in range(groups + 1):
            frequency(k)
            if q and k == groups // 2:
                combine(q - 1)
                if q == last:
                    send_taps(0)
        finish(q)
        trade(q)
    combine(last)
    send_taps(len(sets) - 1)
    send_response(len(sets) - 1)
    send_inputs()
    for g in range(len(sets)):
        pass_taps(g)
        gate_grad(g)
        taps_out(g, m.taps_in, m.lines_in, dp)
        close_taps(g)

    few = pl.ds(0, groups - 1)
    for g in range(len(sets)):
        gg_out(g).wait()
        gf_out(g).wait()
    settle(ogi_ref, m.gi_recv)
    settle(m.stage.at[:, few], m.stage_send)
    settle(m.peaks.at[few], m.peaks_send)
    settle(m.gi.at[few], m.gi_send)
    settle(m.resp.at[few], m.resp_send)
    settle(m.taps.at[few], m.taps_send)
    settle(m.lines.at[few], m.lines_send)
    settle(m.other, m.other_send)
    settle(m.peaks_in, m.peaks_other_send)
    settle(m.inbox, m.trade_send)
    settle(m.taps_in, m.taps_other_send)
    settle(m.lines_in, m.lines_other_send)


def fused(f, x, dy, gate):
    groups, owned, width = f.shape
    parts = PARTS if owned % (32 * PARTS) == 0 else 1
    high, low = tables(groups, width)
    anywhere = pl.BlockSpec(memory_space=pl.ANY)
    shape = (groups, owned, width)
    scratch = buffers(groups, parts, owned, width)
    return pl.pallas_call(
        partial(fused_kernel, groups, parts, tuple(scratch)),
        in_specs=[anywhere] * 6,
        out_specs=[anywhere] * 3,
        out_shape=[
            jax.ShapeDtypeStruct(shape, F32),
            jax.ShapeDtypeStruct(shape, BF16),
            jax.ShapeDtypeStruct(shape, BF16),
        ],
        scratch_shapes=list(scratch.values()),
        compiler_params=pltpu.CompilerParams(
            collective_id=0, has_side_effects=True, vmem_limit_bytes=52 * 1024 * 1024
        ),
    )(high, low, f, x, dy, gate)


def shards(inputs, gate, grad_out, filters):
    groups = lax.axis_size("ctx")
    channels, width = inputs.shape[1:]
    owned = channels // groups

    def blocks(array):
        return array.reshape(groups, owned, width)

    gf, gi, gg = fused(*(blocks(v) for v in (filters, inputs, grad_out, gate)))
    return (
        gi.reshape(1, channels, width),
        gg.reshape(1, channels, width),
        gf.reshape(channels, width),
    )


def solution(mesh):
    placed = (P("dp", "tp", "ctx"), P("dp", "tp", "ctx"), P("dp", "tp", "ctx"), P("tp", "ctx"))
    return jax.shard_map(
        shards,
        mesh=mesh,
        in_specs=placed,
        out_specs=(P("dp", "tp", "ctx"), P("dp", "tp", "ctx"), P("tp", "ctx")),
        check_vma=False,
    )
```

```python
import math
from functools import partial
from types import SimpleNamespace

import jax
import jax.numpy as jnp
import numpy as np
from jax import lax
from jax.experimental import pallas as pl
from jax.experimental.pallas import tpu as pltpu
from jax.sharding import PartitionSpec as P

BF16 = jnp.bfloat16
F32 = jnp.float32
PARTS = 4
SPAN = 250.0
TINY = 1e-35
MESH = pl.DeviceIdType.MESH


def tables(groups, width):
    outer = 2 * groups
    total = outer * width
    freqs = groups + 1
    k1 = np.arange(freqs)[:, None, None]
    b = np.arange(width)[None, :, None]
    k2 = np.arange(width)[None, None, :]
    angle = 2.0 * math.pi * ((b * (k1 + outer * k2)) % total) / total
    cosine, sine = np.cos(angle), -np.sin(angle)
    top = np.concatenate([cosine, sine], axis=2)
    bottom = np.concatenate([-sine, cosine], axis=2)
    matrix = np.concatenate([top, bottom], axis=1).astype(np.float32)
    high = matrix.astype(BF16)
    low = (matrix - high.astype(np.float32)).astype(BF16)
    return high, low


def rotate(value, turn):
    real, imag = value
    eighth = round(turn * 8) % 8 if abs(turn * 8 - round(turn * 8)) < 1e-9 else None
    if eighth == 0:
        return value
    if eighth == 2:
        return -imag, real
    if eighth == 4:
        return -real, -imag
    if eighth == 6:
        return imag, -real
    cosine, sine = math.cos(2.0 * math.pi * turn), math.sin(2.0 * math.pi * turn)
    return real * cosine - imag * sine, real * sine + imag * cosine


def complex_dft(values, sign):
    count = len(values)
    if count == 1:
        return values
    even, odd = complex_dft(values[0::2], sign), complex_dft(values[1::2], sign)
    turned = [rotate(value, sign * i / count) for i, value in enumerate(odd)]
    upper = [(e[0] + t[0], e[1] + t[1]) for e, t in zip(even, turned)]
    lower = [(e[0] - t[0], e[1] - t[1]) for e, t in zip(even, turned)]
    return upper + lower


def odd_dft(values):
    count = len(values)
    if count == 1:
        return [(values[0], None)]
    half = count // 2
    pairs = [rotate((values[i], -values[i + half]), -i / (2 * count)) for i in range(half)]
    found = complex_dft(pairs, -1)
    out = []
    for k in range(1, count, 2):
        if k % 4 == 1:
            out.append(found[(k - 1) // 4])
        else:
            real, imag = found[(2 * count - k - 1) // 4]
            out.append((real, -imag))
    return out


def weave(even, odd):
    out = []
    for i, value in enumerate(even):
        out.append(value)
        if i < len(odd):
            out.append(odd[i])
    return out


def real_dft(values):
    count = len(values)
    if count == 1:
        return [(values[0], None)]
    half = count // 2
    sums = [values[i] + values[i + half] for i in range(half)]
    gaps = [values[i] - values[i + half] for i in range(half)]
    return weave(real_dft(sums), odd_dft(gaps))


def padded_dft(values):
    return weave(real_dft(values), odd_dft(values))


def odd_dft_back(values, count):
    if count == 1:
        return [values[0][0]]
    half = count // 2
    found = []
    for i in range(half):
        k = 4 * i + 1
        if k < count:
            found.append(values[(k - 1) // 2])
        else:
            real, imag = values[(2 * count - k - 1) // 2]
            found.append((real, -imag))
    turned = [rotate(value, i / (2 * count)) for i, value in enumerate(complex_dft(found, 1))]
    return [value[0] for value in turned] + [-value[1] for value in turned]


def real_dft_back(values, count):
    if count == 1:
        return [values[0][0]]
    sums = real_dft_back(values[0::2], count // 2)
    gaps = odd_dft_back(values[1::2], count // 2)
    return [s + g for s, g in zip(sums, gaps)] + [s - g for s, g in zip(sums, gaps)]


def padded_dft_back(values, count):
    whole = real_dft_back(values[0::2], count)
    return [w + o for w, o in zip(whole, odd_dft_back(values[1::2], count))]


def split(value):
    high = value.astype(BF16)
    return high, (value - high.astype(F32)).astype(BF16)


def encode(value):
    peak = jnp.maximum(jnp.max(jnp.abs(value), axis=1, keepdims=True), TINY)
    size = jnp.exp2(jnp.abs(value) * (SPAN / peak) - SPAN / 2)
    return jnp.where(value < 0, -size, size).astype(BF16), peak


def decode(sent, peak):
    sent = sent.astype(F32)
    size = (jnp.log2(jnp.abs(sent)) + SPAN / 2) * (peak * (1.0 / SPAN))
    return jnp.where(sent < 0, -size, size)


def diagonal(rows, base):
    lane = lax.broadcasted_iota(jnp.int32, (rows, 128), 1)
    return lane == lax.broadcasted_iota(jnp.int32, (rows, 128), 0) + base


def collect(peak, base):
    return jnp.sum(jnp.where(diagonal(peak.shape[0], base), peak, 0.0), axis=0, keepdims=True)


def spread(line, rows, base):
    return jnp.sum(jnp.where(diagonal(rows, base), line, 0.0), axis=1, keepdims=True)


def buffers(groups, parts, owned, width):
    chunk = owned // parts
    slim = chunk // 2
    block = max(16, slim)
    tall = 2 * chunk + block
    freqs = groups + 1

    def vm(*shape, kind=BF16):
        return pltpu.VMEM(shape, kind)

    def dma(*shape):
        return pltpu.SemaphoreType.DMA(shape)

    lines = (groups, parts, 1, 128)
    taps = (groups, parts * block, width)
    sets = min(parts, 2)
    return dict(
        mh=vm(freqs, 2 * width, 2 * width),
        ml=vm(freqs, 2 * width, 2 * width),
        dy=vm(groups, owned, width),
        gate=vm(groups, owned, width),
        fin=vm(parts, groups, slim, width, kind=F32),
        stage=vm(parts, groups, tall, width),
        recv=vm(parts, groups, tall, width),
        other=vm(parts, groups, block, width),
        peaks=vm(groups, parts, 128, kind=F32),
        peaks_in=vm(groups, parts, 128, kind=F32),
        peaks_other=vm(groups, parts, 128, kind=F32),
        sig=vm(groups, chunk, width, kind=F32),
        a_hi=vm(freqs, 3 * chunk, 2 * width),
        a_lo=vm(freqs, 3 * chunk, 2 * width),
        b_hi=vm(freqs, 3 * chunk, 2 * width),
        b_lo=vm(freqs, 3 * chunk, 2 * width),
        spec=vm(freqs, 3 * chunk, 2 * width, kind=F32),
        gi=vm(groups, owned, width),
        resp=vm(groups, owned, width),
        resp_in=vm(groups, owned, width),
        gf=vm(parts, groups, chunk, width, kind=F32),
        inbox=vm(parts, groups, slim, width, kind=F32),
        taps=vm(*taps),
        taps_in=vm(*taps),
        taps_other=vm(*taps),
        lines=vm(*lines, kind=F32),
        lines_in=vm(*lines, kind=F32),
        lines_other=vm(*lines, kind=F32),
        gg_out=vm(groups, owned, width),
        gf_out=vm(groups, owned, width, kind=F32),
        load_sem=dma(4),
        x_sem=dma(parts),
        f_sem=dma(parts),
        stage_send=dma(),
        stage_recv=dma(parts),
        other_send=dma(),
        other_recv=dma(parts),
        peaks_send=dma(),
        peaks_recv=dma(),
        peaks_other_send=dma(),
        peaks_other_recv=dma(),
        gi_send=dma(),
        gi_recv=dma(),
        resp_send=dma(),
        resp_recv=dma(sets),
        trade_send=dma(),
        trade_recv=dma(parts),
        taps_send=dma(),
        taps_recv=dma(sets),
        lines_send=dma(),
        lines_recv=dma(sets),
        taps_other_send=dma(),
        taps_other_recv=dma(sets),
        lines_other_send=dma(),
        lines_other_recv=dma(sets),
        gg_sem=dma(sets),
        gf_sem=dma(sets),
    )


def fused_kernel(groups, parts, names, high_ref, low_ref, f_ref, x_ref, dy_ref, gate_ref, ogf_ref, ogi_ref, ogg_ref, *scratch):
    m = SimpleNamespace(**dict(zip(names, scratch)))
    owned, width = f_ref.shape[1:]
    chunk = owned // parts
    slim = chunk // 2
    block = m.other.shape[2]
    rows = min(32, chunk)
    me, dp = lax.axis_index("ctx"), lax.axis_index("dp")
    twin = 1 - dp
    sets = ((0, parts - 1), (parts - 1, 1)) if parts > 1 else ((0, 1),)
    unit = 1.0 / (groups * width)

    def part(q):
        return pl.ds(q * chunk, chunk)

    def remote(source, target, send, recv, device):
        return pltpu.make_async_remote_copy(
            src_ref=source, dst_ref=target, send_sem=send, recv_sem=recv, device_id=device, device_id_type=MESH
        )

    def local(source, target, sem):
        return pltpu.make_async_copy(source, target, sem)

    def settle(ref, sem):
        pltpu.make_async_copy(ref, ref, sem).wait()

    def peers(body):
        def run(o, _):
            body(lax.rem(me + o, groups))
            return 0

        lax.fori_loop(1, groups, run, 0)

    def spray(source, target, send, recv):
        peers(lambda to: remote(source(to), target, send, recv, {"ctx": to}).start())
        local(source(me), target, recv).start()

    def greet():
        barrier = pltpu.get_barrier_semaphore()
        peers(lambda to: pl.semaphore_signal(barrier, inc=1, device_id={"ctx": to}, device_id_type=MESH))
        pl.semaphore_signal(barrier, inc=1, device_id={"dp": twin}, device_id_type=MESH)
        return lambda: pl.semaphore_wait(barrier, groups)

    def loads():
        return (
            local(dy_ref, m.dy, m.load_sem.at[0]),
            local(gate_ref, m.gate, m.load_sem.at[1]),
            *(
                local(f_ref.at[:, pl.ds(pl.multiple_of(q * chunk + dp * slim, slim), slim)], m.fin.at[q], m.f_sem.at[q])
                for q in range(parts)
            ),
            *(local(x_ref.at[:, part(q)], m.stage.at[q, :, pl.ds(0, chunk)], m.x_sem.at[q]) for q in range(parts)),
        )

    def tables_in():
        return local(high_ref, m.mh, m.load_sem.at[2]), local(low_ref, m.ml, m.load_sem.at[3])

    def prepare(a, _):
        found = []
        for q in range(parts):
            line = jnp.zeros((1, 128), F32)
            for at in range(0, chunk, rows):
                here = pl.ds(q * chunk + at, rows)
                sent, peak = encode(m.dy[a, here, :].astype(F32) * m.gate[a, here, :].astype(F32))
                m.stage[q, a, pl.ds(chunk + at, rows), :] = sent
                line = line + collect(peak, at)
            value = m.fin[q, a]
            if block > slim:
                value = jnp.concatenate([value, jnp.zeros((block - slim, width), F32)], axis=0)
            sent, peak = encode(value)
            m.stage[q, a, pl.ds(2 * chunk, block), :] = sent
            found.append(line + collect(peak, chunk))
        m.peaks[a] = jnp.concatenate(found, axis=0)
        return 0

    def inward(q):
        spray(lambda to: m.stage.at[q, to], m.recv.at[q, me], m.stage_send, m.stage_recv.at[q])

    def pass_filters(q):
        settle(m.recv.at[q], m.stage_recv.at[q])
        if 1 <= q + 1 < parts:
            inward(q + 1)
        remote(
            m.recv.at[q, :, pl.ds(2 * chunk, block)], m.other.at[q], m.other_send, m.other_recv.at[q], {"dp": twin}
        ).start()

    def by_rows(body):
        def run(r, _):
            body(pl.multiple_of(r * 16, 16))
            return 0

        lax.fori_loop(0, chunk // 16, run, 0)

    def put(high, low, k, s, at, real, imag):
        to = pl.ds(pl.multiple_of(at + s * chunk, 16), 16)
        if imag is None:
            imag = jnp.zeros_like(real)
        high[k, to, :width], low[k, to, :width] = split(real)
        high[k, to, width:], low[k, to, width:] = split(imag)

    def analyse(s, at, values):
        for k, (real, imag) in enumerate(padded_dft(values)):
            put(m.a_hi, m.a_lo, k, s, at, real, imag)

    def fill(q):
        def signals(at):
            here = pl.ds(at, 16)
            analyse(0, at, [m.recv[q, a, here, :].astype(F32) for a in range(groups)])
            there = pl.ds(pl.multiple_of(chunk + at, 16), 16)
            analyse(
                1,
                at,
                [
                    decode(m.recv[q, a, there, :], spread(m.peaks_in[a, pl.ds(q, 1), :], 16, at) )
                    for a in range(groups)
                ],
            )

        def taps(source, lines, which):
            here = pl.ds(pl.multiple_of(which * slim, slim), slim)
            for a in range(groups):
                peak = spread(lines[a, pl.ds(q, 1), :], block, chunk)
                m.sig[a, here, :] = decode(source(a), peak)[:slim]

        by_rows(signals)
        taps(lambda a: m.recv[q, a, pl.ds(2 * chunk, block), :], m.peaks_in, dp)
        if q == 0:
            settle(m.peaks_other, m.peaks_other_recv)
        settle(m.other.at[q], m.other_recv.at[q])
        taps(lambda a: m.other[q, a], m.peaks_other, twin)
        by_rows(lambda at: analyse(2, at, [m.sig[a, pl.ds(at, 16), :] for a in range(groups)]))

    def frequency(k):
        def multiply(high, low, contract):
            dims = (((1,), (contract,)), ((), ()))
            dot = partial(lax.dot_general, dimension_numbers=dims, preferred_element_type=F32)
            high, low = high[k], low[k]
            both = dot(jnp.concatenate([high, low], axis=0), m.mh[k])
            return both[: 3 * chunk] + both[3 * chunk :] + dot(high, m.ml[k])

        found = multiply(m.a_hi, m.a_lo, 0)
        (xr, xi), (pr, pi), (fr, fi) = (
            (found[s * chunk : (s + 1) * chunk, :width], found[s * chunk : (s + 1) * chunk, width:]) for s in range(3)
        )
        for s, (real, imag) in enumerate(
            (
                (fr * xr - fi * xi, fr * xi + fi * xr),
                (fr * pr + fi * pi, fr * pi - fi * pr),
                (xr * pr + xi * pi, xr * pi - xi * pr),
            )
        ):
            to = pl.ds(s * chunk, chunk)
            m.b_hi[k, to, :width], m.b_lo[k, to, :width] = split(real)
            m.b_hi[k, to, width:], m.b_lo[k, to, width:] = split(imag)
        m.spec[k] = multiply(m.b_hi, m.b_lo, 1)

    def frequencies():
        step = 3 if (groups + 1) % 3 == 0 else 1

        def some_k(i, _):
            for j in range(step):
                frequency(i * step + j)
            return 0

        lax.fori_loop(0, (groups + 1) // step, some_k, 0)

    def synthesise(s, at):
        to = pl.ds(pl.multiple_of(at + s * chunk, 16), 16)
        values = [(m.spec[k, to, :width], m.spec[k, to, width:]) for k in range(groups + 1)]
        values[0], values[-1] = ((value[0] * 0.5, None) for value in (values[0], values[-1]))
        return padded_dft_back(values, groups)

    def finish_taps(q):
        def one(at):
            for a, value in enumerate(synthesise(2, at)):
                m.gf[q, a, pl.ds(at, 16), :] = value * unit

        by_rows(one)

    def finish_out(q):
        m.lines[:, q] = jnp.zeros((groups, 1, 128), F32)

        def one(at):
            here = pl.ds(pl.multiple_of(q * chunk + at, 16), 16)
            for a, value in enumerate(synthesise(0, at)):
                sent, peak = encode(value * unit)
                m.resp[a, here, :] = sent
                m.lines[a, q] += collect(peak, at)
            for a, value in enumerate(synthesise(1, at)):
                m.gi[a, here, :] = (value * unit).astype(BF16)

        by_rows(one)

    def trade(q):
        remote(
            m.gf.at[q, :, pl.ds(pl.multiple_of(twin * slim, slim), slim)],
            m.inbox.at[q],
            m.trade_send,
            m.trade_recv.at[q],
            {"dp": twin},
        ).start()

    def send_response(g):
        here = span(g)
        spray(lambda to: m.resp.at[to, here], m.resp_in.at[me, here], m.resp_send, m.resp_recv.at[g])

    def send_inputs():
        spray(lambda to: m.gi.at[to], ogi_ref.at[me], m.gi_send, m.gi_recv)

    def combine(q):
        settle(m.inbox.at[q], m.trade_recv.at[q])

        def one(a, _):
            value = m.gf[q, a, pl.ds(pl.multiple_of(dp * slim, slim), slim), :] + m.inbox[q, a]
            if block > slim:
                value = jnp.concatenate([value, jnp.zeros((block - slim, width), F32)], axis=0)
            sent, peak = encode(value)
            m.taps[a, pl.ds(q * block, block), :] = sent
            m.lines[a, q] += collect(peak, chunk)
            return 0

        lax.fori_loop(0, groups, one, 0)

    def some(g):
        first, count = sets[g]
        return pl.ds(first, count)

    def span(g):
        first, count = sets[g]
        return pl.ds(first * chunk, count * chunk)

    def span_taps(g):
        first, count = sets[g]
        return pl.ds(first * block, count * block)

    def send_taps(g):
        here, there = some(g), span_taps(g)
        spray(lambda to: m.lines.at[to, here], m.lines_in.at[me, here], m.lines_send, m.lines_recv.at[g])
        spray(lambda to: m.taps.at[to, there], m.taps_in.at[me, there], m.taps_send, m.taps_recv.at[g])

    def pass_taps(g):
        lines, taps = m.lines_in.at[:, some(g)], m.taps_in.at[:, span_taps(g)]
        settle(lines, m.lines_recv.at[g])
        settle(taps, m.taps_recv.at[g])
        other_lines, other_taps = m.lines_other.at[:, some(g)], m.taps_other.at[:, span_taps(g)]
        remote(lines, other_lines, m.lines_other_send, m.lines_other_recv.at[g], {"dp": twin}).start()
        remote(taps, other_taps, m.taps_other_send, m.taps_other_recv.at[g], {"dp": twin}).start()

    def gg_out(g):
        return local(m.gg_out.at[:, span(g)], ogg_ref.at[:, span(g)], m.gg_sem.at[g])

    def gf_out(g):
        return local(m.gf_out.at[:, span(g)], ogf_ref.at[:, span(g)], m.gf_sem.at[g])

    def gate_grad(g):
        settle(m.resp_in.at[:, span(g)], m.resp_recv.at[g])
        first, count = sets[g]

        def one(a, _):
            for q in range(first, first + count):
                for at in range(0, chunk, rows):
                    here = pl.ds(q * chunk + at, rows)
                    value = decode(m.resp_in[a, here, :], spread(m.lines_in[a, q], rows, at))
                    m.gg_out[a, here, :] = (m.dy[a, here, :].astype(F32) * value).astype(BF16)
            return 0

        lax.fori_loop(0, groups, one, 0)
        gg_out(g).start()

    def taps_out(g, source, lines, which):
        first, count = sets[g]

        def one(a, _):
            for q in range(first, first + count):
                value = decode(source[a, pl.ds(q * block, block), :], spread(lines[a, q], block, chunk))
                here = pl.ds(pl.multiple_of(q * chunk + which * slim, slim), slim)
                m.gf_out[a, here, :] = value[:slim]
            return 0

        lax.fori_loop(0, groups, one, 0)

    def close_taps(g):
        settle(m.taps_other.at[:, span_taps(g)], m.taps_other_recv.at[g])
        settle(m.lines_other.at[:, some(g)], m.lines_other_recv.at[g])
        taps_out(g, m.taps_other, m.lines_other, twin)
        gf_out(g).start()

    entered = greet()
    for copy in (*loads(), *tables_in()):
        copy.start()
    for copy in loads():
        copy.wait()
    lax.fori_loop(0, groups, prepare, 0)
    entered()
    spray(lambda to: m.peaks.at[to], m.peaks_in.at[me], m.peaks_send, m.peaks_recv)
    for q in range(min(1, parts)):
        inward(q)
    for copy in tables_in():
        copy.wait()
    settle(m.peaks_in, m.peaks_recv)
    remote(m.peaks_in, m.peaks_other, m.peaks_other_send, m.peaks_other_recv, {"dp": twin}).start()

    last = parts - 1
    for q in range(parts):
        pass_filters(q)
        if q and q == last:
            send_response(0)
        fill(q)
        if q:
            combine(q - 1)
            if q == last:
                send_taps(0)
        frequencies()
        finish_taps(q)
        trade(q)
        finish_out(q)
    combine(last)
    send_taps(len(sets) - 1)
    send_response(len(sets) - 1)
    send_inputs()
    for g in range(len(sets)):
        pass_taps(g)
        gate_grad(g)
        taps_out(g, m.taps_in, m.lines_in, dp)
        close_taps(g)

    few = pl.ds(0, groups - 1)
    for g in range(len(sets)):
        gg_out(g).wait()
        gf_out(g).wait()
    settle(ogi_ref, m.gi_recv)
    settle(m.stage.at[:, few], m.stage_send)
    settle(m.peaks.at[few], m.peaks_send)
    settle(m.gi.at[few], m.gi_send)
    settle(m.resp.at[few], m.resp_send)
    settle(m.taps.at[few], m.taps_send)
    settle(m.lines.at[few], m.lines_send)
    settle(m.other, m.other_send)
    settle(m.peaks_in, m.peaks_other_send)
    settle(m.inbox, m.trade_send)
    settle(m.taps_in, m.taps_other_send)
    settle(m.lines_in, m.lines_other_send)


def fused(f, x, dy, gate):
    groups, owned, width = f.shape
    parts = PARTS if owned % (32 * PARTS) == 0 else 1
    high, low = tables(groups, width)
    anywhere = pl.BlockSpec(memory_space=pl.ANY)
    shape = (groups, owned, width)
    scratch = buffers(groups, parts, owned, width)
    return pl.pallas_call(
        partial(fused_kernel, groups, parts, tuple(scratch)),
        in_specs=[anywhere] * 6,
        out_specs=[anywhere] * 3,
        out_shape=[
            jax.ShapeDtypeStruct(shape, F32),
            jax.ShapeDtypeStruct(shape, BF16),
            jax.ShapeDtypeStruct(shape, BF16),
        ],
        scratch_shapes=list(scratch.values()),
        compiler_params=pltpu.CompilerParams(
            collective_id=0, has_side_effects=True, vmem_limit_bytes=52 * 1024 * 1024
        ),
    )(high, low, f, x, dy, gate)


def shards(inputs, gate, grad_out, filters):
    groups = lax.axis_size("ctx")
    channels, width = inputs.shape[1:]
    owned = channels // groups

    def blocks(array):
        return array.reshape(groups, owned, width)

    gf, gi, gg = fused(*(blocks(v) for v in (filters, inputs, grad_out, gate)))
    return (
        gi.reshape(1, channels, width),
        gg.reshape(1, channels, width),
        gf.reshape(channels, width),
    )


def solution(mesh):
    placed = (P("dp", "tp", "ctx"), P("dp", "tp", "ctx"), P("dp", "tp", "ctx"), P("tp", "ctx"))
    return jax.shard_map(
        shards,
        mesh=mesh,
        in_specs=placed,
        out_specs=(P("dp", "tp", "ctx"), P("dp", "tp", "ctx"), P("tp", "ctx")),
        check_vma=False,
    )
```

```python
import math
from functools import partial
from types import SimpleNamespace

import jax
import jax.numpy as jnp
import numpy as np
from jax import lax
from jax.experimental import pallas as pl
from jax.experimental.pallas import tpu as pltpu
from jax.sharding import PartitionSpec as P

BF16 = jnp.bfloat16
F32 = jnp.float32
PARTS = 4
SPAN = 250.0
TINY = 1e-35
MESH = pl.DeviceIdType.MESH


def tables(groups, width):
    outer = 2 * groups
    total = outer * width
    freqs = groups + 1
    k1 = np.arange(freqs)[:, None, None]
    b = np.arange(width)[None, :, None]
    k2 = np.arange(width)[None, None, :]
    angle = 2.0 * math.pi * ((b * (k1 + outer * k2)) % total) / total
    cosine, sine = np.cos(angle), -np.sin(angle)
    top = np.concatenate([cosine, sine], axis=2)
    bottom = np.concatenate([-sine, cosine], axis=2)
    matrix = np.concatenate([top, bottom], axis=1).astype(np.float32)
    high = matrix.astype(BF16)
    low = (matrix - high.astype(np.float32)).astype(BF16)
    return high, low


def rotate(value, turn):
    real, imag = value
    eighth = round(turn * 8) % 8 if abs(turn * 8 - round(turn * 8)) < 1e-9 else None
    if eighth == 0:
        return value
    if eighth == 2:
        return -imag, real
    if eighth == 4:
        return -real, -imag
    if eighth == 6:
        return imag, -real
    cosine, sine = math.cos(2.0 * math.pi * turn), math.sin(2.0 * math.pi * turn)
    return real * cosine - imag * sine, real * sine + imag * cosine


def complex_dft(values, sign):
    count = len(values)
    if count == 1:
        return values
    even, odd = complex_dft(values[0::2], sign), complex_dft(values[1::2], sign)
    turned = [rotate(value, sign * i / count) for i, value in enumerate(odd)]
    upper = [(e[0] + t[0], e[1] + t[1]) for e, t in zip(even, turned)]
    lower = [(e[0] - t[0], e[1] - t[1]) for e, t in zip(even, turned)]
    return upper + lower


def odd_dft(values):
    count = len(values)
    if count == 1:
        return [(values[0], None)]
    half = count // 2
    pairs = [rotate((values[i], -values[i + half]), -i / (2 * count)) for i in range(half)]
    found = complex_dft(pairs, -1)
    out = []
    for k in range(1, count, 2):
        if k % 4 == 1:
            out.append(found[(k - 1) // 4])
        else:
            real, imag = found[(2 * count - k - 1) // 4]
            out.append((real, -imag))
    return out


def weave(even, odd):
    out = []
    for i, value in enumerate(even):
        out.append(value)
        if i < len(odd):
            out.append(odd[i])
    return out


def real_dft(values):
    count = len(values)
    if count == 1:
        return [(values[0], None)]
    half = count // 2
    sums = [values[i] + values[i + half] for i in range(half)]
    gaps = [values[i] - values[i + half] for i in range(half)]
    return weave(real_dft(sums), odd_dft(gaps))


def padded_dft(values):
    return weave(real_dft(values), odd_dft(values))


def odd_dft_back(values, count):
    if count == 1:
        return [values[0][0]]
    half = count // 2
    found = []
    for i in range(half):
        k = 4 * i + 1
        if k < count:
            found.append(values[(k - 1) // 2])
        else:
            real, imag = values[(2 * count - k - 1) // 2]
            found.append((real, -imag))
    turned = [rotate(value, i / (2 * count)) for i, value in enumerate(complex_dft(found, 1))]
    return [value[0] for value in turned] + [-value[1] for value in turned]


def real_dft_back(values, count):
    if count == 1:
        return [values[0][0]]
    sums = real_dft_back(values[0::2], count // 2)
    gaps = odd_dft_back(values[1::2], count // 2)
    return [s + g for s, g in zip(sums, gaps)] + [s - g for s, g in zip(sums, gaps)]


def padded_dft_back(values, count):
    whole = real_dft_back(values[0::2], count)
    return [w + o for w, o in zip(whole, odd_dft_back(values[1::2], count))]


def split(value):
    high = value.astype(BF16)
    return high, (value - high.astype(F32)).astype(BF16)


def encode(value):
    peak = jnp.maximum(jnp.max(jnp.abs(value), axis=1, keepdims=True), TINY)
    size = jnp.exp2(jnp.abs(value) * (SPAN / peak) - SPAN / 2)
    return jnp.where(value < 0, -size, size).astype(BF16), peak


def decode(sent, peak):
    sent = sent.astype(F32)
    size = (jnp.log2(jnp.abs(sent)) + SPAN / 2) * (peak * (1.0 / SPAN))
    return jnp.where(sent < 0, -size, size)


def diagonal(rows, base):
    lane = lax.broadcasted_iota(jnp.int32, (rows, 128), 1)
    return lane == lax.broadcasted_iota(jnp.int32, (rows, 128), 0) + base


def collect(peak, base):
    return jnp.sum(jnp.where(diagonal(peak.shape[0], base), peak, 0.0), axis=0, keepdims=True)


def spread(line, rows, base):
    return jnp.sum(jnp.where(diagonal(rows, base), line, 0.0), axis=1, keepdims=True)


def buffers(groups, parts, owned, width):
    chunk = owned // parts
    slim = chunk // 2
    block = max(16, slim)
    tall = 2 * chunk + block
    freqs = groups + 1

    def vm(*shape, kind=BF16):
        return pltpu.VMEM(shape, kind)

    def dma(*shape):
        return pltpu.SemaphoreType.DMA(shape)

    lines = (groups, parts, 1, 128)
    taps = (groups, parts * block, width)
    sets = min(parts, 2)
    return dict(
        mh=vm(freqs, 2 * width, 2 * width),
        ml=vm(freqs, 2 * width, 2 * width),
        dy=vm(groups, owned, width),
        gate=vm(groups, owned, width),
        fin=vm(parts, groups, slim, width, kind=F32),
        stage=vm(parts, groups, tall, width),
        recv=vm(parts, groups, tall, width),
        other=vm(parts, groups, block, width),
        peaks=vm(groups, parts, 128, kind=F32),
        peaks_in=vm(groups, parts, 128, kind=F32),
        peaks_other=vm(groups, parts, 128, kind=F32),
        sig=vm(groups, chunk, width, kind=F32),
        a_hi=vm(freqs, 3 * chunk, 2 * width),
        a_lo=vm(freqs, 3 * chunk, 2 * width),
        b_hi=vm(freqs, 3 * chunk, 2 * width),
        b_lo=vm(freqs, 3 * chunk, 2 * width),
        spec=vm(freqs, 3 * chunk, 2 * width, kind=F32),
        gi=vm(groups, owned, width),
        resp=vm(groups, owned, width),
        resp_in=vm(groups, owned, width),
        gf=vm(parts, groups, chunk, width, kind=F32),
        inbox=vm(parts, groups, slim, width, kind=F32),
        taps=vm(*taps),
        taps_in=vm(*taps),
        taps_other=vm(*taps),
        lines=vm(*lines, kind=F32),
        lines_in=vm(*lines, kind=F32),
        lines_other=vm(*lines, kind=F32),
        gg_out=vm(groups, owned, width),
        gf_out=vm(groups, owned, width, kind=F32),
        load_sem=dma(4),
        x_sem=dma(parts),
        f_sem=dma(parts),
        stage_send=dma(),
        stage_recv=dma(parts),
        other_send=dma(),
        other_recv=dma(parts),
        peaks_send=dma(),
        peaks_recv=dma(),
        peaks_other_send=dma(),
        peaks_other_recv=dma(),
        gi_send=dma(),
        gi_recv=dma(),
        resp_send=dma(),
        resp_recv=dma(sets),
        trade_send=dma(),
        trade_recv=dma(parts),
        taps_send=dma(),
        taps_recv=dma(sets),
        lines_send=dma(),
        lines_recv=dma(sets),
        taps_other_send=dma(),
        taps_other_recv=dma(sets),
        lines_other_send=dma(),
        lines_other_recv=dma(sets),
        gg_sem=dma(sets),
        gf_sem=dma(sets),
    )


def fused_kernel(groups, parts, names, high_ref, low_ref, f_ref, x_ref, dy_ref, gate_ref, ogf_ref, ogi_ref, ogg_ref, *scratch):
    m = SimpleNamespace(**dict(zip(names, scratch)))
    owned, width = f_ref.shape[1:]
    chunk = owned // parts
    slim = chunk // 2
    block = m.other.shape[2]
    rows = min(32, chunk)
    me, dp = lax.axis_index("ctx"), lax.axis_index("dp")
    twin = 1 - dp
    sets = ((0, parts - 1), (parts - 1, 1)) if parts > 1 else ((0, 1),)
    unit = 1.0 / (groups * width)

    def part(q):
        return pl.ds(q * chunk, chunk)

    def remote(source, target, send, recv, device):
        return pltpu.make_async_remote_copy(
            src_ref=source, dst_ref=target, send_sem=send, recv_sem=recv, device_id=device, device_id_type=MESH
        )

    def local(source, target, sem):
        return pltpu.make_async_copy(source, target, sem)

    def settle(ref, sem):
        pltpu.make_async_copy(ref, ref, sem).wait()

    def peers(body):
        def run(o, _):
            body(lax.rem(me + o, groups))
            return 0

        lax.fori_loop(1, groups, run, 0)

    def spray(source, target, send, recv):
        peers(lambda to: remote(source(to), target, send, recv, {"ctx": to}).start())
        local(source(me), target, recv).start()

    def greet():
        barrier = pltpu.get_barrier_semaphore()
        peers(lambda to: pl.semaphore_signal(barrier, inc=1, device_id={"ctx": to}, device_id_type=MESH))
        pl.semaphore_signal(barrier, inc=1, device_id={"dp": twin}, device_id_type=MESH)
        return lambda: pl.semaphore_wait(barrier, groups)

    def loads():
        return (
            local(dy_ref, m.dy, m.load_sem.at[0]),
            local(gate_ref, m.gate, m.load_sem.at[1]),
            *(
                local(f_ref.at[:, pl.ds(pl.multiple_of(q * chunk + dp * slim, slim), slim)], m.fin.at[q], m.f_sem.at[q])
                for q in range(parts)
            ),
            *(local(x_ref.at[:, part(q)], m.stage.at[q, :, pl.ds(0, chunk)], m.x_sem.at[q]) for q in range(parts)),
        )

    def tables_in():
        return local(high_ref, m.mh, m.load_sem.at[2]), local(low_ref, m.ml, m.load_sem.at[3])

    def prepare(a, _):
        found = []
        for q in range(parts):
            line = jnp.zeros((1, 128), F32)
            for at in range(0, chunk, rows):
                here = pl.ds(q * chunk + at, rows)
                sent, peak = encode(m.dy[a, here, :].astype(F32) * m.gate[a, here, :].astype(F32))
                m.stage[q, a, pl.ds(chunk + at, rows), :] = sent
                line = line + collect(peak, at)
            value = m.fin[q, a]
            if block > slim:
                value = jnp.concatenate([value, jnp.zeros((block - slim, width), F32)], axis=0)
            sent, peak = encode(value)
            m.stage[q, a, pl.ds(2 * chunk, block), :] = sent
            found.append(line + collect(peak, chunk))
        m.peaks[a] = jnp.concatenate(found, axis=0)
        return 0

    def inward(q):
        spray(lambda to: m.stage.at[q, to], m.recv.at[q, me], m.stage_send, m.stage_recv.at[q])

    def pass_filters(q):
        settle(m.recv.at[q], m.stage_recv.at[q])
        if 1 <= q + 1 < parts:
            inward(q + 1)
        remote(
            m.recv.at[q, :, pl.ds(2 * chunk, block)], m.other.at[q], m.other_send, m.other_recv.at[q], {"dp": twin}
        ).start()

    def by_rows(body):
        def run(r, _):
            body(pl.multiple_of(r * 16, 16))
            return 0

        lax.fori_loop(0, chunk // 16, run, 0)

    def put(high, low, k, s, at, real, imag):
        to = pl.ds(pl.multiple_of(at + s * chunk, 16), 16)
        if imag is None:
            imag = jnp.zeros_like(real)
        high[k, to, :width], low[k, to, :width] = split(real)
        high[k, to, width:], low[k, to, width:] = split(imag)

    def analyse(s, at, values):
        for k, (real, imag) in enumerate(padded_dft(values)):
            put(m.a_hi, m.a_lo, k, s, at, real, imag)

    def fill(q):
        def signals(at):
            here = pl.ds(at, 16)
            analyse(0, at, [m.recv[q, a, here, :].astype(F32) for a in range(groups)])
            there = pl.ds(pl.multiple_of(chunk + at, 16), 16)
            analyse(
                1,
                at,
                [
                    decode(m.recv[q, a, there, :], spread(m.peaks_in[a, pl.ds(q, 1), :], 16, at) )
                    for a in range(groups)
                ],
            )

        def taps(source, lines, which):
            here = pl.ds(pl.multiple_of(which * slim, slim), slim)
            for a in range(groups):
                peak = spread(lines[a, pl.ds(q, 1), :], block, chunk)
                m.sig[a, here, :] = decode(source(a), peak)[:slim]

        by_rows(signals)
        taps(lambda a: m.recv[q, a, pl.ds(2 * chunk, block), :], m.peaks_in, dp)
        if q == 0:
            settle(m.peaks_other, m.peaks_other_recv)
        settle(m.other.at[q], m.other_recv.at[q])
        taps(lambda a: m.other[q, a], m.peaks_other, twin)
        by_rows(lambda at: analyse(2, at, [m.sig[a, pl.ds(at, 16), :] for a in range(groups)]))

    def frequency(k):
        def multiply(high, low, contract):
            dims = (((1,), (contract,)), ((), ()))
            dot = partial(lax.dot_general, dimension_numbers=dims, preferred_element_type=F32)
            high, low = high[k], low[k]
            both = dot(jnp.concatenate([high, low], axis=0), m.mh[k])
            return both[: 3 * chunk] + both[3 * chunk :] + dot(high, m.ml[k])

        found = multiply(m.a_hi, m.a_lo, 0)
        (xr, xi), (pr, pi), (fr, fi) = (
            (found[s * chunk : (s + 1) * chunk, :width], found[s * chunk : (s + 1) * chunk, width:]) for s in range(3)
        )
        for s, (real, imag) in enumerate(
            (
                (fr * xr - fi * xi, fr * xi + fi * xr),
                (fr * pr + fi * pi, fr * pi - fi * pr),
                (xr * pr + xi * pi, xr * pi - xi * pr),
            )
        ):
            to = pl.ds(s * chunk, chunk)
            m.b_hi[k, to, :width], m.b_lo[k, to, :width] = split(real)
            m.b_hi[k, to, width:], m.b_lo[k, to, width:] = split(imag)
        m.spec[k] = multiply(m.b_hi, m.b_lo, 1)

    def frequencies():
        step = 3 if (groups + 1) % 3 == 0 else 1

        def some_k(i, _):
            for j in range(step):
                frequency(i * step + j)
            return 0

        lax.fori_loop(0, (groups + 1) // step, some_k, 0)

    def synthesise(s, at):
        to = pl.ds(pl.multiple_of(at + s * chunk, 16), 16)
        values = [(m.spec[k, to, :width], m.spec[k, to, width:]) for k in range(groups + 1)]
        values[0], values[-1] = ((value[0] * 0.5, None) for value in (values[0], values[-1]))
        return padded_dft_back(values, groups)

    def finish_taps(q):
        def one(at):
            for a, value in enumerate(synthesise(2, at)):
                m.gf[q, a, pl.ds(at, 16), :] = value * unit

        by_rows(one)

    def finish_out(q):
        m.lines[:, q] = jnp.zeros((groups, 1, 128), F32)

        def one(at):
            here = pl.ds(pl.multiple_of(q * chunk + at, 16), 16)
            for a, value in enumerate(synthesise(0, at)):
                sent, peak = encode(value * unit)
                m.resp[a, here, :] = sent
                m.lines[a, q] += collect(peak, at)
            for a, value in enumerate(synthesise(1, at)):
                m.gi[a, here, :] = (value * unit).astype(BF16)

        by_rows(one)

    def trade(q):
        remote(
            m.gf.at[q, :, pl.ds(pl.multiple_of(twin * slim, slim), slim)],
            m.inbox.at[q],
            m.trade_send,
            m.trade_recv.at[q],
            {"dp": twin},
        ).start()

    def send_response(g):
        here = span(g)
        spray(lambda to: m.resp.at[to, here], m.resp_in.at[me, here], m.resp_send, m.resp_recv.at[g])

    def send_inputs():
        spray(lambda to: m.gi.at[to], ogi_ref.at[me], m.gi_send, m.gi_recv)

    def in_pairs(body):
        step = 4 if groups % 4 == 0 else 1

        def run(i, _):
            for j in range(step):
                body(i * step + j)
            return 0

        lax.fori_loop(0, groups // step, run, 0)

    def combine(q):
        settle(m.inbox.at[q], m.trade_recv.at[q])

        def one(a):
            value = m.gf[q, a, pl.ds(pl.multiple_of(dp * slim, slim), slim), :] + m.inbox[q, a]
            if block > slim:
                value = jnp.concatenate([value, jnp.zeros((block - slim, width), F32)], axis=0)
            sent, peak = encode(value)
            m.taps[a, pl.ds(q * block, block), :] = sent
            m.lines[a, q] += collect(peak, chunk)

        in_pairs(one)

    def some(g):
        first, count = sets[g]
        return pl.ds(first, count)

    def span(g):
        first, count = sets[g]
        return pl.ds(first * chunk, count * chunk)

    def span_taps(g):
        first, count = sets[g]
        return pl.ds(first * block, count * block)

    def send_taps(g):
        here, there = some(g), span_taps(g)
        spray(lambda to: m.lines.at[to, here], m.lines_in.at[me, here], m.lines_send, m.lines_recv.at[g])
        spray(lambda to: m.taps.at[to, there], m.taps_in.at[me, there], m.taps_send, m.taps_recv.at[g])

    def pass_taps(g):
        lines, taps = m.lines_in.at[:, some(g)], m.taps_in.at[:, span_taps(g)]
        settle(lines, m.lines_recv.at[g])
        settle(taps, m.taps_recv.at[g])
        other_lines, other_taps = m.lines_other.at[:, some(g)], m.taps_other.at[:, span_taps(g)]
        remote(lines, other_lines, m.lines_other_send, m.lines_other_recv.at[g], {"dp": twin}).start()
        remote(taps, other_taps, m.taps_other_send, m.taps_other_recv.at[g], {"dp": twin}).start()

    def gg_out(g):
        return local(m.gg_out.at[:, span(g)], ogg_ref.at[:, span(g)], m.gg_sem.at[g])

    def gf_out(g):
        return local(m.gf_out.at[:, span(g)], ogf_ref.at[:, span(g)], m.gf_sem.at[g])

    def gate_grad(g):
        settle(m.resp_in.at[:, span(g)], m.resp_recv.at[g])
        first, count = sets[g]

        def one(a):
            for q in range(first, first + count):
                for at in range(0, chunk, rows):
                    here = pl.ds(q * chunk + at, rows)
                    value = decode(m.resp_in[a, here, :], spread(m.lines_in[a, q], rows, at))
                    m.gg_out[a, here, :] = (m.dy[a, here, :].astype(F32) * value).astype(BF16)

        in_pairs(one)
        gg_out(g).start()

    def taps_out(g, source, lines, which):
        first, count = sets[g]

        def one(a):
            for q in range(first, first + count):
                value = decode(source[a, pl.ds(q * block, block), :], spread(lines[a, q], block, chunk))
                here = pl.ds(pl.multiple_of(q * chunk + which * slim, slim), slim)
                m.gf_out[a, here, :] = value[:slim]

        in_pairs(one)

    def close_taps(g):
        settle(m.taps_other.at[:, span_taps(g)], m.taps_other_recv.at[g])
        settle(m.lines_other.at[:, some(g)], m.lines_other_recv.at[g])
        taps_out(g, m.taps_other, m.lines_other, twin)
        gf_out(g).start()

    entered = greet()
    for copy in (*loads(), *tables_in()):
        copy.start()
    for copy in loads():
        copy.wait()
    lax.fori_loop(0, groups, prepare, 0)
    entered()
    spray(lambda to: m.peaks.at[to], m.peaks_in.at[me], m.peaks_send, m.peaks_recv)
    for q in range(min(1, parts)):
        inward(q)
    for copy in tables_in():
        copy.wait()
    settle(m.peaks_in, m.peaks_recv)
    remote(m.peaks_in, m.peaks_other, m.peaks_other_send, m.peaks_other_recv, {"dp": twin}).start()

    last = parts - 1
    for q in range(parts):
        pass_filters(q)
        if q and q == last:
            send_response(0)
        fill(q)
        if q:
            combine(q - 1)
            if q == last:
                send_taps(0)
        frequencies()
        finish_taps(q)
        trade(q)
        finish_out(q)
    combine(last)
    send_taps(len(sets) - 1)
    send_response(len(sets) - 1)
    send_inputs()
    for g in range(len(sets)):
        pass_taps(g)
        gate_grad(g)
        taps_out(g, m.taps_in, m.lines_in, dp)
        close_taps(g)

    few = pl.ds(0, groups - 1)
    for g in range(len(sets)):
        gg_out(g).wait()
        gf_out(g).wait()
    settle(ogi_ref, m.gi_recv)
    settle(m.stage.at[:, few], m.stage_send)
    settle(m.peaks.at[few], m.peaks_send)
    settle(m.gi.at[few], m.gi_send)
    settle(m.resp.at[few], m.resp_send)
    settle(m.taps.at[few], m.taps_send)
    settle(m.lines.at[few], m.lines_send)
    settle(m.other, m.other_send)
    settle(m.peaks_in, m.peaks_other_send)
    settle(m.inbox, m.trade_send)
    settle(m.taps_in, m.taps_other_send)
    settle(m.lines_in, m.lines_other_send)


def fused(f, x, dy, gate):
    groups, owned, width = f.shape
    parts = PARTS if owned % (32 * PARTS) == 0 else 1
    high, low = tables(groups, width)
    anywhere = pl.BlockSpec(memory_space=pl.ANY)
    shape = (groups, owned, width)
    scratch = buffers(groups, parts, owned, width)
    return pl.pallas_call(
        partial(fused_kernel, groups, parts, tuple(scratch)),
        in_specs=[anywhere] * 6,
        out_specs=[anywhere] * 3,
        out_shape=[
            jax.ShapeDtypeStruct(shape, F32),
            jax.ShapeDtypeStruct(shape, BF16),
            jax.ShapeDtypeStruct(shape, BF16),
        ],
        scratch_shapes=list(scratch.values()),
        compiler_params=pltpu.CompilerParams(
            collective_id=0, has_side_effects=True, vmem_limit_bytes=53 * 1024 * 1024
        ),
    )(high, low, f, x, dy, gate)


def shards(inputs, gate, grad_out, filters):
    groups = lax.axis_size("ctx")
    channels, width = inputs.shape[1:]
    owned = channels // groups

    def blocks(array):
        return array.reshape(groups, owned, width)

    gf, gi, gg = fused(*(blocks(v) for v in (filters, inputs, grad_out, gate)))
    return (
        gi.reshape(1, channels, width),
        gg.reshape(1, channels, width),
        gf.reshape(channels, width),
    )


def solution(mesh):
    placed = (P("dp", "tp", "ctx"), P("dp", "tp", "ctx"), P("dp", "tp", "ctx"), P("tp", "ctx"))
    return jax.shard_map(
        shards,
        mesh=mesh,
        in_specs=placed,
        out_specs=(P("dp", "tp", "ctx"), P("dp", "tp", "ctx"), P("tp", "ctx")),
        check_vma=False,
    )
```
